32 devices in a mesh: dp: 16 (over z, x, core), tp: 2 (over y).
Axes of the slice: x: 2, y: 2, z: 4, core: 2. Of those that a mesh axis runs over, the one named last changes fastest.
Arguments:
- tokens: bfloat16 [8192, 768], P('dp'), may hold values from -6 to 6
- neighbours: bfloat16 [128, 128, 768], P('dp'), may hold values from -6 to 6
- out_grad: bfloat16 [8192, 768], P('dp'), may hold values from -6 to 6
- group_sizes: int32 [16], P('dp'), may hold values from 1 to 4, as said below
- seq_lengths: int32 [16, 4], P('dp'), may hold values from 0 to 512, as said below
- stretch_neighbours: int32 [128, 2], P('dp'), may hold values from 0 to 7, as said below
- norm_gain: float32 [3, 768], replicated, may hold values from 0.5 to 1.5
- norm_bias: float32 [3, 768], replicated, may hold values from -1 to 1
- self_qkv_w: bfloat16 [768, 3, 768], P(None, None, 'tp'), may hold values from -0.3125 to 0.3125
- self_qkv_b: float32 [3, 768], P(None, 'tp'), may hold values from -1 to 1
- self_out_w: bfloat16 [768, 768], P('tp'), may hold values from -0.875 to 0.875
- self_out_b: float32 [768], replicated, may hold values from -1 to 1
- cross_q_w: bfloat16 [768, 768], P(None, 'tp'), may hold values from -0.3125 to 0.3125
- cross_q_b: float32 [768], P('tp'), may hold values from -1 to 1
- cross_kv_w: bfloat16 [768, 2, 768], P(None, None, 'tp'), may hold values from -0.3125 to 0.3125
- cross_v_b: float32 [768], P('tp'), may hold values from -1 to 1
- cross_out_w: bfloat16 [768, 768], P('tp'), may hold values from -0.875 to 0.875
- cross_out_b: float32 [768], replicated, may hold values from -1 to 1
- mlp_in_w: bfloat16 [768, 3072], P(None, 'tp'), may hold values from -0.21875 to 0.21875
- mlp_in_b: float32 [3072], P('tp'), may hold values from -1 to 1
- mlp_out_w: bfloat16 [3072, 768], P('tp'), may hold values from -0.21875 to 0.21875
- mlp_out_b: float32 [768], replicated, may hold values from -1 to 1
Outputs:
- output: bfloat16 [8192, 768], P('dp', 'tp')
- tokens_grad: bfloat16 [8192, 768], P('dp', 'tp')
- neighbours_grad: bfloat16 [128, 128, 768], P('dp', None, 'tp')
- norm_gain_grad: float32 [3, 768], replicated
- norm_bias_grad: float32 [3, 768], replicated
- self_qkv_w_grad: float32 [768, 3, 768], P('dp', None, 'tp')
- self_qkv_b_grad: float32 [3, 768], P(None, 'tp')
- self_out_w_grad: float32 [768, 768], P('tp', 'dp')
- self_out_b_grad: float32 [768], replicated
- cross_q_w_grad: float32 [768, 768], P('dp', 'tp')
- cross_q_b_grad: float32 [768], P('tp')
- cross_kv_w_grad: float32 [768, 2, 768], P('dp', None, 'tp')
- cross_v_b_grad: float32 [768], P('tp')
- cross_out_w_grad: float32 [768, 768], P('tp', 'dp')
- cross_out_b_grad: float32 [768], replicated
- mlp_in_w_grad: float32 [768, 3072], P('dp', 'tp')
- mlp_in_b_grad: float32 [3072], P('tp')
- mlp_out_w_grad: float32 [3072, 768], P('tp', 'dp')
- mlp_out_b_grad: float32 [768], replicated
The draws below stay inside these ranges and needn't reach their ends.
Inputs may be any that keep to these rules, and one draw needn't show every extreme that they name: `group_sizes`: a power of two; bucket b's padded sequence length is 512 // group_sizes[b]; some device has 1 and some has 4 in every draw. `seq_lengths`: slots at or beyond the device's group size are 0; the others lie between a quarter of the padded length and the padded length; the first slot of every device is exactly its padded length. `stretch_neighbours`: indices into the owning device's own 8 stored neighbours; the two of a block differ.
All inputs are finite; a program needn't handle non-finite values.
Results may differ from the reference program's by a relative error of at most 0.024.
The reference program's roundings to bfloat16 on the way count: a program that leaves them out, or rounds other values in their place, can miss the bound.
Values sent between devices are 32-bit elements; how exact they have to be, the bound alone decides.
No kernel may reach another device: no remote copies, remote signals or barrier semaphores. Data moves between devices by JAX's collectives and lax.ppermute only.
A program may use at most 192 MiB of HBM per device.

```python
import math
import jax
import jax.numpy as jnp
from jax import lax

D = 768
FF = 3072
HEAD_DIM = 64
STRETCH = 64
NEIGH_LEN = 128
MAX_SEQS = 4
TOK_DEV = 512
NEIGH_DEV = 8
TOKENS = 8192
NEIGHBOURS = 128
N_DP = 16


def bucket_groups(key):
    picked = jax.random.randint(jax.random.fold_in(key, 11), (N_DP,), 0, 8)
    groups = jnp.where(picked == 0, 1, jnp.where(picked < 4, 2, 4)).astype(jnp.int32)
    order = jax.random.permutation(jax.random.fold_in(key, 12), N_DP)
    groups = groups.at[order[0]].set(1)
    groups = groups.at[order[1]].set(MAX_SEQS)
    return groups


def draw_group_sizes(key, part):
    return bucket_groups(key)


def draw_seq_lengths(key, part):
    groups = bucket_groups(key)
    padded = TOK_DEV // groups
    lowest = padded // 4
    raw_draw = jax.random.randint(jax.random.fold_in(key, 13), (N_DP, MAX_SEQS), 0, 1 << 20)
    lengths = lowest[:, None] + raw_draw % (padded - lowest + 1)[:, None]
    slot_ids = jnp.arange(MAX_SEQS, dtype=jnp.int32)
    lengths = jnp.where(slot_ids[None, :] == 0, padded[:, None], lengths)
    lengths = jnp.where(slot_ids[None, :] < groups[:, None], lengths, 0)
    return lengths.astype(jnp.int32)


def draw_stretch_neighbours(key, part):
    total_rows = N_DP * (TOK_DEV // STRETCH)
    first_pick = jax.random.randint(jax.random.fold_in(key, 21), (total_rows,), 0, NEIGH_DEV)
    step_pick = jax.random.randint(jax.random.fold_in(key, 22), (total_rows,), 1, NEIGH_DEV)
    second_pick = (first_pick + step_pick) % NEIGH_DEV
    chosen = jax.random.randint(jax.random.fold_in(key, 23), (), 0, total_rows)
    first_pick = first_pick.at[chosen].set(0)
    second_pick = second_pick.at[chosen].set(NEIGH_DEV - 1)
    return jnp.stack([first_pick, second_pick], axis=1).astype(jnp.int32)


def levels(rng, dims, pieces, low, high):
    level, own = 1.0, jax.random.fold_in(rng, 6)
    for axis_at, parts in pieces:
        steps = jnp.exp(jax.random.uniform(jax.random.fold_in(own, axis_at), (parts,), jnp.float32, low / len(pieces), high / len(pieces)))
        level = level * jnp.repeat(steps, dims[axis_at] // parts).reshape([-1 if axis == axis_at else 1 for axis in range(len(dims))])
    return level


def centred(own_key, extent, scale, reach, pieces=(), kind=jnp.bfloat16):
    entries = scale * jax.random.normal(own_key, extent, jnp.float32)
    if pieces:
        entries = entries * levels(own_key, extent, pieces, -0.22, 0.18)
    return jnp.clip(entries, -reach, reach).astype(kind)


def setup_inputs(seed: int = 0) -> dict:
    splits = jax.random.split(jax.random.key(seed), 23)
    tokens = centred(splits[0], (TOKENS, D), 1.0, 6.0, ((0, 16),))
    neighbours = centred(splits[1], (NEIGHBOURS, NEIGH_LEN, D), 1.0, 6.0, ((0, 16),))
    out_grad = centred(splits[2], (TOKENS, D), 1.0, 6.0, ((0, 16),))
    group_sizes = draw_group_sizes(jax.random.fold_in(splits[22], 71), 0)
    seq_lengths = draw_seq_lengths(jax.random.fold_in(splits[22], 71), 0)
    stretch_neighbours = draw_stretch_neighbours(jax.random.fold_in(splits[22], 71), 0)
    norm_gain = jnp.clip(1.0 + 0.1 * jax.random.normal(splits[6], (3, D), jnp.float32), 0.5, 1.5)
    norm_bias = centred(splits[7], (3, D), 0.2, 1.0, (), jnp.float32)
    self_qkv_w = centred(splits[8], (D, 3, D), (D // 2) ** -0.5, 0.3125, ((2, 2),))
    self_qkv_b = centred(splits[9], (3, D), 0.2, 1.0, ((1, 2),), jnp.float32)
    self_out_w = centred(splits[10], (D, D), (D // 16) ** -0.5, 0.875, ((0, 2),))
    self_out_b = centred(splits[11], (D,), 0.2, 1.0, (), jnp.float32)
    cross_q_w = centred(splits[12], (D, D), (D // 2) ** -0.5, 0.3125, ((1, 2),))
    cross_q_b = centred(splits[13], (D,), 0.2, 1.0, ((0, 2),), jnp.float32)
    cross_kv_w = centred(splits[14], (D, 2, D), (D // 2) ** -0.5, 0.3125, ((2, 2),))
    cross_v_b = centred(splits[15], (D,), 0.2, 1.0, ((0, 2),), jnp.float32)
    cross_out_w = centred(splits[16], (D, D), (D // 16) ** -0.5, 0.875, ((0, 2),))
    cross_out_b = centred(splits[17], (D,), 0.2, 1.0, (), jnp.float32)
    mlp_in_w = centred(splits[18], (D, FF), D ** -0.5, 0.21875, ((1, 2),))
    mlp_in_b = centred(splits[19], (FF,), 0.2, 1.0, ((0, 2),), jnp.float32)
    mlp_out_w = centred(splits[20], (FF, D), (FF // 4) ** -0.5, 0.21875, ((0, 2),))
    mlp_out_b = centred(splits[21], (D,), 0.2, 1.0, (), jnp.float32)
    return {"tokens": tokens, "neighbours": neighbours, "out_grad": out_grad, "group_sizes": group_sizes, "seq_lengths": seq_lengths, "stretch_neighbours": stretch_neighbours, "norm_gain": norm_gain, "norm_bias": norm_bias, "self_qkv_w": self_qkv_w, "self_qkv_b": self_qkv_b, "self_out_w": self_out_w, "self_out_b": self_out_b, "cross_q_w": cross_q_w, "cross_q_b": cross_q_b, "cross_kv_w": cross_kv_w, "cross_v_b": cross_v_b, "cross_out_w": cross_out_w, "cross_out_b": cross_out_b, "mlp_in_w": mlp_in_w, "mlp_in_b": mlp_in_b, "mlp_out_w": mlp_out_w, "mlp_out_b": mlp_out_b}


@jax.custom_vjp
def low(v):
    return lax.optimization_barrier(v.astype(jnp.bfloat16)).astype(jnp.float32)

@jax.custom_vjp
def low_back(v):
    return v

def low_keep(v):
    return (low(v), None)

def low_pass(kept, grad):
    return (grad,)

def back_keep(v):
    return (v, None)

def back_low(kept, grad):
    return (low(grad),)
low.defvjp(low_keep, low_pass)
low_back.defvjp(back_keep, back_low)
highest = lax.Precision.HIGHEST

def layer_norm(field, gain, shift):
    center = field - lax.optimization_barrier(jnp.mean(field, axis=-1, keepdims=True))
    spread = lax.optimization_barrier(jnp.mean(center * center, axis=-1, keepdims=True))
    return center * lax.rsqrt(spread + 1e-05) * gain + shift

def rotate(field, position):
    halfway = HEAD_DIM // 2
    frequency = jnp.exp(-math.log(10000.0) * jnp.arange(halfway, dtype=jnp.float32) / halfway)
    angles = position.astype(jnp.float32)[:, None] * frequency[None, :]
    cosine = jnp.cos(angles)[:, None, :]
    sine_part = jnp.sin(angles)[:, None, :]
    shaped = field.reshape(field.shape[0], -1, HEAD_DIM)
    first_half = shaped[..., :halfway]
    second_half = shaped[..., halfway:]
    turned = jnp.concatenate([first_half * cosine - second_half * sine_part, second_half * cosine + first_half * sine_part], axis=-1)
    return turned.reshape(field.shape)

def device_forward(tokens, store, groups, lengths, assigned, params):
    norm_gain, norm_bias, self_qkv_w, self_qkv_b, self_out_w, self_out_b, cross_q_w, cross_q_b, cross_kv_w, cross_v_b, cross_out_w, cross_out_b, mlp_in_w, mlp_in_b, mlp_out_w, mlp_out_b = params
    count = tokens.shape[0]
    width = tokens.shape[1]
    heads = width // HEAD_DIM
    padded = count // groups
    row_ids = jnp.arange(count, dtype=jnp.int32)
    position = row_ids % padded
    sequence = row_ids // padded
    slot_ids = jnp.arange(lengths.shape[0], dtype=jnp.int32)
    tok_len = lax.optimization_barrier(jnp.sum(jnp.where(sequence[:, None] == slot_ids[None, :], lengths[None, :], 0), axis=1))
    allowed = (sequence[:, None] == sequence[None, :]) & (position[None, :] <= position[:, None]) & (position[None, :] < tok_len[None, :])
    shifted = position + (STRETCH - 1)
    valid = ((shifted < padded) & (shifted < tok_len)).astype(tokens.dtype)[:, None]
    ln_one = low(layer_norm(tokens, norm_gain[0], norm_bias[0]))
    qkv_pre = low_back(jnp.einsum('td,dcf->tcf', ln_one, self_qkv_w, precision=highest) + self_qkv_b)
    query = low(rotate(qkv_pre[:, 0], position)).reshape(count, heads, HEAD_DIM)
    key_rows = low(rotate(qkv_pre[:, 1], position)).reshape(count, heads, HEAD_DIM)
    value_rows = low(qkv_pre[:, 2]).reshape(count, heads, HEAD_DIM)
    scores = low_back(jnp.einsum('qhd,khd->hqk', query, key_rows, precision=highest) * 0.125)
    scores = jnp.where(allowed[None], scores, -1e+30)
    probs = low(jax.nn.softmax(scores, axis=-1))
    mixed = jnp.einsum('hqk,khd->qhd', probs, value_rows, precision=highest).reshape(count, width)
    mixed = low(low_back(mixed))
    attn = low_back(jnp.dot(mixed, self_out_w, precision=highest) + self_out_b)
    hidden_one = tokens + attn
    ln_two = low(layer_norm(hidden_one, norm_gain[1], norm_bias[1]))
    cross_query = low(low_back(jnp.dot(ln_two, cross_q_w, precision=highest) + cross_q_b))
    kv_bias = jnp.stack([jnp.zeros_like(cross_v_b), cross_v_b])
    flat_store = store.reshape(-1, width)
    store_kv = low_back(jnp.einsum('nd,dcf->ncf', flat_store, cross_kv_w, precision=highest) + kv_bias)
    store_keys = low(store_kv[:, 0]).reshape(store.shape[0], store.shape[1], heads, HEAD_DIM)
    store_values = low(store_kv[:, 1]).reshape(store.shape[0], store.shape[1], heads, HEAD_DIM)
    stretches = assigned.shape[0]
    block_keys = store_keys[assigned].reshape(stretches, 2 * store.shape[1], heads, HEAD_DIM)
    block_values = store_values[assigned].reshape(stretches, 2 * store.shape[1], heads, HEAD_DIM)
    query_rows = jnp.roll(cross_query, -(STRETCH - 1), axis=0).reshape(stretches, STRETCH, heads, HEAD_DIM)
    cross_scores = low_back(jnp.einsum('cqhd,ckhd->chqk', query_rows, block_keys, precision=highest) * 0.125)
    cross_probs = low(jax.nn.softmax(cross_scores, axis=-1))
    cross_rows = jnp.einsum('chqk,ckhd->cqhd', cross_probs, block_values, precision=highest).reshape(count, width)
    cross_mix = low(low_back(jnp.roll(cross_rows * valid, STRETCH - 1, axis=0)))
    cross = low_back(jnp.dot(cross_mix, cross_out_w, precision=highest) + cross_out_b)
    hidden_two = hidden_one + cross
    ln_three = low(layer_norm(hidden_two, norm_gain[2], norm_bias[2]))
    pre_act = low_back(jnp.dot(ln_three, mlp_in_w, precision=highest) + mlp_in_b)
    act = low(jax.nn.gelu(pre_act, approximate=False))
    mlp = low_back(jnp.dot(act, mlp_out_w, precision=highest) + mlp_out_b)
    return hidden_two + mlp

def reference(tokens, neighbours, out_grad, group_sizes, seq_lengths, stretch_neighbours, norm_gain, norm_bias, self_qkv_w, self_qkv_b, self_out_w, self_out_b, cross_q_w, cross_q_b, cross_kv_w, cross_v_b, cross_out_w, cross_out_b, mlp_in_w, mlp_in_b, mlp_out_w, mlp_out_b):
    params = tuple((weight.astype(jnp.float32) for weight in (norm_gain, norm_bias, self_qkv_w, self_qkv_b, self_out_w, self_out_b, cross_q_w, cross_q_b, cross_kv_w, cross_v_b, cross_out_w, cross_out_b, mlp_in_w, mlp_in_b, mlp_out_w, mlp_out_b)))
    token_blocks = tokens.astype(jnp.float32).reshape(N_DP, TOK_DEV, D)
    store_blocks = neighbours.astype(jnp.float32).reshape(N_DP, NEIGH_DEV, NEIGH_LEN, D)
    grad_blocks = out_grad.astype(jnp.float32).reshape(N_DP, TOK_DEV, D)
    assigned_blocks = stretch_neighbours.reshape(N_DP, TOK_DEV // STRETCH, 2)

    def one_device(totals, inputs):
        block, store, cotangent, groups, lengths, assigned = inputs

        def forward(block, store, params):
            return device_forward(block, store, groups, lengths, assigned, params)
        result, pullback = jax.vjp(forward, block, store, params)
        block_grad, store_grad, param_grads = pullback(cotangent)
        totals = jax.tree.map(jnp.add, totals, param_grads)
        return (totals, (result.astype(jnp.bfloat16), block_grad.astype(jnp.bfloat16), store_grad.astype(jnp.bfloat16)))
    totals, stacked = lax.scan(one_device, jax.tree.map(jnp.zeros_like, params), (token_blocks, store_blocks, grad_blocks, group_sizes, seq_lengths, assigned_blocks))
    outputs, block_grads, store_grads = stacked
    return (outputs.reshape(TOKENS, D), block_grads.reshape(TOKENS, D), store_grads.reshape(NEIGHBOURS, NEIGH_LEN, D), totals[0], totals[1], totals[2], totals[3], totals[4], totals[5], totals[6], totals[7], totals[8], totals[9], totals[10], totals[11], totals[12], totals[13], totals[14], totals[15])
```

```python
from functools import partial
import math

import jax
import jax.numpy as jnp
from jax import lax
from jax.experimental import pallas as pl
from jax.experimental.pallas import tpu as pltpu
from jax.sharding import PartitionSpec as P

HEAD_DIM = 64
STRETCH = 64
LANES = 128
F32 = jnp.float32
BF16 = jnp.bfloat16
TILE = 128


def dot(left, right):
    return lax.dot_general(left, right, (((1,), (0,)), ((), ())), preferred_element_type=F32)


def dot_t(left, right):
    return lax.dot_general(left, right, (((1,), (1,)), ((), ())), preferred_element_type=F32)


def tdot(left, right):
    return lax.dot_general(left, right, (((0,), (0,)), ((), ())), preferred_element_type=F32)


def norm_stats(field):
    center = field - jnp.mean(field, axis=-1, keepdims=True)
    spread = jnp.mean(center * center, axis=-1, keepdims=True)
    scale = lax.rsqrt(spread + 1e-05)
    return center * scale, scale


def norm_back(xhat, scale, gain, gradient):
    scaled = gradient * gain
    first = jnp.mean(scaled, axis=-1, keepdims=True)
    second = jnp.mean(scaled * xhat, axis=-1, keepdims=True)
    return scale * (scaled - first - xhat * second)


def lane_ids(rows):
    return lax.broadcasted_iota(jnp.int32, (rows, LANES), 1)


def turn(field, cosine, sine, direction):
    lane = lane_ids(field.shape[0])
    ahead = pltpu.roll(field, LANES - HEAD_DIM // 2, 1)
    behind = pltpu.roll(field, HEAD_DIM // 2, 1)
    crossed = jnp.where((lane & (HEAD_DIM - 1)) < HEAD_DIM // 2, -ahead, behind)
    return field * cosine + crossed * (sine * direction)


def two_heads(field):
    low = lane_ids(field.shape[0]) < HEAD_DIM
    zero = jnp.zeros_like(field)
    return jnp.concatenate([jnp.where(low, field, zero), jnp.where(low, zero, field)], axis=0)


def join_heads(field):
    half = field.shape[0] // 2
    return jnp.where(lane_ids(half) < HEAD_DIM, field[:half], field[half:])


def two_columns(columns, first):
    lane = lane_ids(columns.shape[0])
    parts = [
        jnp.sum(jnp.where(lane == first + head, columns, 0.0), axis=-1, keepdims=True)
        for head in range(2)
    ]
    return jnp.concatenate(parts, axis=0)


def put_columns(columns, values, first):
    half = columns.shape[0]
    lane = lane_ids(half)
    columns = jnp.where(lane == first, values[:half], columns)
    return jnp.where(lane == first + 1, values[half:], columns)


def slot_length(ids, info, slots):
    length = jnp.zeros_like(ids)
    for slot in range(slots):
        length = jnp.where(ids >= slot * info[0], info[3 + slot], length)
    return length


def fill_mask(bias_ref, info, slots):
    count = bias_ref.shape[0]
    padded = info[0]
    for start in range(0, count, TILE):
        shape = (TILE, start + TILE)
        rows = lax.broadcasted_iota(jnp.int32, shape, 0) + start
        keys = lax.broadcasted_iota(jnp.int32, shape, 1)
        place = keys & (padded - 1)
        allowed = (
            (keys <= rows)
            & (keys >= rows - (rows & (padded - 1)))
            & (place < slot_length(keys, info, slots))
        )
        bias_ref[start : start + TILE, : start + TILE] = jnp.where(allowed, 0.0, -1e30)


def valid_rows(count, info, slots):
    rows = lax.broadcasted_iota(jnp.int32, (count, LANES), 0)
    shifted = (rows & (info[0] - 1)) + (STRETCH - 1)
    return (shifted < info[0]) & (shifted < slot_length(rows, info, slots))


def join_peer(peer_ref, near_ref, far_ref, core):
    half = near_ref.shape[0]
    peer_ref[pl.ds(pl.multiple_of(core * half, 64), half), :] = near_ref[...].astype(BF16)
    peer_ref[pl.ds(pl.multiple_of((1 - core) * half, 64), half), :] = far_ref[...].astype(BF16)


def self_forward(slots, info, tok, weight, bias, gain, shift, cosine, sine, ln_out, qkv_out, mix_out, lse_out, mask_out):
    count = tok.shape[0]
    pairs = weight.shape[2] // LANES
    fill_mask(mask_out, info, slots)
    step = 256

    def project(index, carry):
        rows = pl.ds(pl.multiple_of(index * step, step), step)
        xhat, _ = norm_stats(tok[rows, :].astype(F32))
        ln = (xhat * gain[...] + shift[...]).astype(BF16)
        ln_out[rows, :] = ln
        for part in range(3):
            made = dot(ln, weight[part]) + bias[part : part + 1, :]
            for pair in range(pairs):
                piece = made[:, pair * LANES : (pair + 1) * LANES]
                if part < 2:
                    piece = turn(piece, cosine[rows, :], sine[rows, :], 1.0)
                qkv_out[part * pairs + pair, rows, :] = piece.astype(BF16)
        return carry

    lax.fori_loop(0, count // step, project, 0)

    def attend(pair, carry):
        columns = pl.ds(pl.multiple_of(pair * LANES, LANES), LANES)
        for start in range(0, count, TILE):
            rows = slice(start, start + TILE)
            span = slice(0, start + TILE)
            query = two_heads(qkv_out[pair, rows, :] * BF16(0.125))
            scores = dot_t(query, qkv_out[pairs + pair, span, :])
            mask = mask_out[rows, span]
            scores = scores + jnp.concatenate([mask, mask], axis=0)
            top = jnp.max(scores, axis=-1, keepdims=True)
            expo = jnp.exp(scores - top)
            total = jnp.sum(expo, axis=-1, keepdims=True)
            probs = (expo * (1.0 / total)).astype(BF16)
            mixed = join_heads(dot(probs, qkv_out[2 * pairs + pair, span, :]))
            mix_out[rows, columns] = mixed.astype(BF16).astype(F32)
            lse_out[rows, :] = put_columns(lse_out[rows, :], top + jnp.log(total), 2 * pair)
        return carry

    lax.fori_loop(0, pairs, attend, 0)


def cross_forward(
    slots, span, info, picks, tok, mix_own, mix_peer, w_own, w_near, w_far, out_bias, gain, shift, q_w, q_b, kv,
    hidden_out, ln_out, query_out, mix_out, lse_out, w_peer, field,
):
    count = tok.shape[0]
    local = q_w.shape[1]
    pairs = local // LANES
    join_peer(w_peer, w_near, w_far, info[2])
    step = 256

    def project(index, carry):
        rows = pl.ds(pl.multiple_of(index * step, step), step)
        attn = dot(mix_own[rows, :].astype(BF16), w_own[...]) + dot(
            mix_peer[rows, :].astype(BF16), w_peer[...]
        )
        hidden = tok[rows, :].astype(F32) + (attn + out_bias[...])
        hidden_out[rows, :] = hidden
        xhat, _ = norm_stats(hidden)
        ln = (xhat * gain[...] + shift[...]).astype(BF16)
        ln_out[rows, :] = ln
        field[rows, :] = dot(ln, q_w[...]) + q_b[...]
        return carry

    lax.fori_loop(0, count // step, project, 0)
    for pair in range(pairs):
        columns = slice(pair * LANES, (pair + 1) * LANES)
        query_out[:, columns] = pltpu.roll(field[:, columns], count - (STRETCH - 1), 0).astype(BF16)

    def block(index, carry):
        rows = pl.ds(pl.multiple_of(index * STRETCH, STRETCH), STRETCH)
        near = pl.ds(pl.multiple_of(picks[index, 0] * span, span), span)
        far = pl.ds(pl.multiple_of(picks[index, 1] * span, span), span)
        lse = jnp.zeros((STRETCH, LANES), F32)
        for pair in range(pairs):
            columns = slice(pair * LANES, (pair + 1) * LANES)
            values = slice(local + pair * LANES, local + (pair + 1) * LANES)
            query = two_heads(query_out[rows, columns] * BF16(0.125))
            keys = jnp.concatenate([kv[near, columns], kv[far, columns]], axis=0)
            vals = jnp.concatenate([kv[near, values], kv[far, values]], axis=0)
            scores = dot_t(query, keys)
            top = jnp.max(scores, axis=-1, keepdims=True)
            expo = jnp.exp(scores - top)
            total = jnp.sum(expo, axis=-1, keepdims=True)
            probs = (expo * (1.0 / total)).astype(BF16)
            field[rows, columns] = join_heads(dot(probs, vals))
            lse = put_columns(lse, top + jnp.log(total), 2 * pair)
        lse_out[rows, :] = lse
        return carry

    lax.fori_loop(0, picks.shape[0], block, 0)
    valid = valid_rows(count, info, slots)
    for pair in range(pairs):
        columns = slice(pair * LANES, (pair + 1) * LANES)
        kept = jnp.where(valid, field[:, columns], 0.0)
        mix_out[:, columns] = pltpu.roll(kept, STRETCH - 1, 0).astype(BF16).astype(F32)


def gelu_parts(field):
    upper = 0.5 * (1.0 + lax.erf(field * (1.0 / math.sqrt(2.0))))
    density = jnp.exp(field * field * -0.5) * (1.0 / math.sqrt(2.0 * math.pi))
    return field * upper, upper + field * density


def feed_forward(
    info, hidden_one, mix_own, mix_peer, w_own, w_near, w_far, out_bias, gain, shift, in_w, in_b, out_w, end_bias, grad,
    hidden_out, ln_out, act_out, pre_out, keep_out, send_out, part_out, bias_out, w_peer,
):
    @pl.when(pl.program_id(0) == 0)
    def _():
        join_peer(w_peer, w_near, w_far, info[2])
        bias_out[...] = jnp.zeros_like(bias_out)

    half = keep_out.shape[1]
    own = pl.ds(pl.multiple_of(info[1] * half, LANES), half)
    peer = pl.ds(pl.multiple_of((1 - info[1]) * half, LANES), half)
    cross = dot(mix_own[...].astype(BF16), w_own[...]) + dot(mix_peer[...].astype(BF16), w_peer[...])
    hidden = hidden_one[...] + (cross + out_bias[...])
    hidden_out[...] = hidden
    xhat, _ = norm_stats(hidden)
    ln = (xhat * gain[...] + shift[...]).astype(BF16)
    ln_out[...] = ln
    act, slope = gelu_parts(dot(ln, in_w[...]) + in_b[...])
    act = act.astype(BF16)
    act_out[...] = act
    grad_pre = (dot_t(grad[...], out_w[...]) * slope).astype(BF16)
    pre_out[...] = grad_pre
    bias_out[...] += jnp.sum(grad_pre.astype(F32), axis=0, keepdims=True)
    part_out[...] = dot_t(grad_pre, in_w[...])
    keep_out[...] = dot(act, out_w[:, own]) + (hidden_out[:, own] + end_bias[:, own])
    send_out[...] = dot(act, out_w[:, peer])


def cross_backward(
    slots, span, info, picks, part_own, part_peer, hidden, out_grad, gain, out_w, query, kv, lse,
    grad_out, low_out, query_out, query_low, store_out, gain_out, shift_out, bias_out, q_bias_out, v_bias_out,
    rows_grad, field, store,
):
    count = hidden.shape[0]
    local = query.shape[1]
    pairs = local // LANES
    step = 256
    gain_out[...] = jnp.zeros_like(gain_out)
    shift_out[...] = jnp.zeros_like(shift_out)
    bias_out[...] = jnp.zeros_like(bias_out)
    store[...] = jnp.zeros_like(store)

    def project(index, carry):
        rows = pl.ds(pl.multiple_of(index * step, step), step)
        gradient = part_own[rows, :] + part_peer[rows, :]
        xhat, scale = norm_stats(hidden[rows, :])
        gain_out[...] += jnp.sum(gradient * xhat, axis=0, keepdims=True)
        shift_out[...] += jnp.sum(gradient, axis=0, keepdims=True)
        two = out_grad[rows, :].astype(F32) + norm_back(xhat, scale, gain[...], gradient)
        grad_out[rows, :] = two
        low = two.astype(BF16)
        low_out[rows, :] = low
        bias_out[...] += jnp.sum(low.astype(F32), axis=0, keepdims=True)
        field[rows, :] = dot_t(low, out_w[...])
        return carry

    lax.fori_loop(0, count // step, project, 0)
    valid = valid_rows(count, info, slots)
    for pair in range(pairs):
        columns = slice(pair * LANES, (pair + 1) * LANES)
        moved = pltpu.roll(field[:, columns].astype(BF16).astype(F32), count - (STRETCH - 1), 0)
        rows_grad[:, columns] = jnp.where(valid, moved, 0.0).astype(BF16)

    def block(index, carry):
        rows = pl.ds(pl.multiple_of(index * STRETCH, STRETCH), STRETCH)
        near = pl.ds(pl.multiple_of(picks[index, 0] * span, span), span)
        far = pl.ds(pl.multiple_of(picks[index, 1] * span, span), span)
        logs = lse[rows, :]
        for pair in range(pairs):
            columns = slice(pair * LANES, (pair + 1) * LANES)
            values = slice(local + pair * LANES, local + (pair + 1) * LANES)
            query_two = two_heads(query[rows, columns] * BF16(0.125))
            grad_two = two_heads(rows_grad[rows, columns])
            keys = jnp.concatenate([kv[near, columns], kv[far, columns]], axis=0)
            vals = jnp.concatenate([kv[near, values], kv[far, values]], axis=0)
            probs = jnp.exp(dot_t(query_two, keys) - two_columns(logs, 2 * pair))
            grad_probs = dot_t(grad_two, vals)
            delta = jnp.sum(probs * grad_probs, axis=-1, keepdims=True)
            grad_scores = (probs * (grad_probs - delta)).astype(BF16)
            field[rows, columns] = join_heads(dot(grad_scores, keys)) * 0.125
            grad_keys = tdot(grad_scores, query_two)
            grad_vals = tdot(probs.astype(BF16), grad_two)
            store[near, columns] += grad_keys[:span]
            store[far, columns] += grad_keys[span:]
            store[near, values] += grad_vals[:span]
            store[far, values] += grad_vals[span:]
        return carry

    lax.fori_loop(0, picks.shape[0], block, 0)
    for pair in range(pairs):
        columns = slice(pair * LANES, (pair + 1) * LANES)
        low = pltpu.roll(field[:, columns], STRETCH - 1, 0).astype(BF16)
        query_low[:, columns] = low
        query_out[:, columns] = low.astype(F32)
        q_bias_out[:, columns] = jnp.sum(low.astype(F32), axis=0, keepdims=True)

    v_bias_out[...] = jnp.zeros_like(v_bias_out)

    def flush(index, carry):
        rows = pl.ds(pl.multiple_of(index * span, span), span)
        low = store[rows, :].astype(BF16)
        store_out[rows, :] = low
        v_bias_out[...] += jnp.sum(low[:, local:].astype(F32), axis=0, keepdims=True)
        return carry

    lax.fori_loop(0, store.shape[0] // span, flush, 0)


def self_backward(
    info, query_own, query_peer, q_w, q_near, q_far, hidden, grad_two, gain_two, out_w, qkv, lse, mask, cosine, sine, w,
    tok, gain_one,
    low_out, qkv_out, keep_out, send_out, sums_out, q_bias_out, q_peer, one, mix_grad, key_grad, value_grad, part,
):
    count = tok.shape[0]
    local = out_w.shape[0]
    pairs = local // LANES
    step = 256
    join_peer(q_peer, q_near, q_far, info[2])
    sums_out[...] = jnp.zeros_like(sums_out)
    half = keep_out.shape[1]
    own = pl.ds(pl.multiple_of(info[1] * half, LANES), half)
    peer = pl.ds(pl.multiple_of((1 - info[1]) * half, LANES), half)

    def project(index, carry):
        rows = pl.ds(pl.multiple_of(index * step, step), step)
        gradient = dot_t(query_own[rows, :], q_w[...]) + dot_t(
            query_peer[rows, :].astype(BF16), q_peer[...]
        )
        xhat, scale = norm_stats(hidden[rows, :])
        sums_out[0:1, :] += jnp.sum(gradient * xhat, axis=0, keepdims=True)
        sums_out[1:2, :] += jnp.sum(gradient, axis=0, keepdims=True)
        grad_one = grad_two[rows, :] + norm_back(xhat, scale, gain_two[...], gradient)
        one[rows, :] = grad_one
        low = grad_one.astype(BF16)
        low_out[rows, :] = low
        sums_out[2:3, :] += jnp.sum(low.astype(F32), axis=0, keepdims=True)
        mixed = dot_t(low, out_w[...])
        for pair in range(pairs):
            mix_grad[pair, rows, :] = mixed[:, pair * LANES : (pair + 1) * LANES].astype(BF16)
        return carry

    lax.fori_loop(0, count // step, project, 0)

    def attend(pair, carry):
        key_grad[...] = jnp.zeros_like(key_grad)
        value_grad[...] = jnp.zeros_like(value_grad)
        for start in range(0, count, TILE):
            rows = slice(start, start + TILE)
            until = slice(0, start + TILE)
            query = two_heads(qkv[pair, rows, :] * BF16(0.125))
            keys = qkv[pairs + pair, until, :]
            vals = qkv[2 * pairs + pair, until, :]
            grad_mix = two_heads(mix_grad[pair, rows, :])
            allowed = mask[rows, until]
            scores = dot_t(query, keys) + jnp.concatenate([allowed, allowed], axis=0)
            probs = jnp.exp(scores - two_columns(lse[rows, :], 2 * pair))
            grad_probs = dot_t(grad_mix, vals)
            delta = jnp.sum(probs * grad_probs, axis=-1, keepdims=True)
            grad_scores = (probs * (grad_probs - delta)).astype(BF16)
            grad_query = join_heads(dot(grad_scores, keys)) * 0.125
            back = turn(grad_query, cosine[rows, :], sine[rows, :], -1.0)
            qkv_out[pair, rows, :] = back.astype(BF16)
            key_grad[until, :] += tdot(grad_scores, query)
            value_grad[until, :] += tdot(probs.astype(BF16), grad_mix)
        for start in range(0, count, TILE):
            rows = slice(start, start + TILE)
            back = turn(key_grad[rows, :], cosine[rows, :], sine[rows, :], -1.0)
            qkv_out[pairs + pair, rows, :] = back.astype(BF16)
            qkv_out[2 * pairs + pair, rows, :] = value_grad[rows, :].astype(BF16)
        return carry

    lax.fori_loop(0, pairs, attend, 0)

    for piece in range(3 * pairs):
        q_bias_out[:, piece * LANES : (piece + 1) * LANES] = jnp.sum(
            qkv_out[piece].astype(F32), axis=0, keepdims=True
        )

    def finish(index, carry):
        rows = pl.ds(pl.multiple_of(index * step, step), step)
        gradient = jnp.zeros((step, tok.shape[1]), F32)
        for part_at in range(3):
            joined = jnp.concatenate(
                [qkv_out[part_at * pairs + pair, rows, :] for pair in range(pairs)], axis=1
            )
            gradient = gradient + dot_t(joined, w[part_at])
        xhat, scale = norm_stats(tok[rows, :].astype(F32))
        sums_out[3:4, :] += jnp.sum(gradient * xhat, axis=0, keepdims=True)
        sums_out[4:5, :] += jnp.sum(gradient, axis=0, keepdims=True)
        part[...] = norm_back(xhat, scale, gain_one[...], gradient)
        keep_out[rows, :] = part[:, own] + one[rows, own]
        send_out[rows, :] = part[:, peer]
        return carry

    lax.fori_loop(0, count // step, finish, 0)


def whole(count):
    return [pl.BlockSpec(memory_space=pltpu.VMEM)] * count


def scalars(count):
    return [pl.BlockSpec(memory_space=pltpu.SMEM)] * count


def shape(dims, kind=F32):
    return jax.ShapeDtypeStruct(dims, kind)


def call(body, name, small, big, outs, scratch=()):
    return pl.pallas_call(
        body,
        name=name,
        out_shape=outs,
        in_specs=scalars(len(small)) + whole(len(big)),
        out_specs=whole(len(outs)),
        scratch_shapes=scratch,
    )(*small, *big)


def per_device(
    tokens,
    neighbours,
    out_grad,
    group_sizes,
    seq_lengths,
    stretch_neighbours,
    norm_gain,
    norm_bias,
    self_qkv_w,
    self_qkv_b,
    self_out_w,
    self_out_b,
    cross_q_w,
    cross_q_b,
    cross_kv_w,
    cross_v_b,
    cross_out_w,
    cross_out_b,
    mlp_in_w,
    mlp_in_b,
    mlp_out_w,
    mlp_out_b,
):
    count, width = tokens.shape
    local = self_qkv_w.shape[2]
    hidden = mlp_in_w.shape[1]
    pairs = local // LANES
    stored, span = neighbours.shape[:2]
    slots = seq_lengths.shape[1]
    dp_size = lax.axis_size("dp")
    tp_at = lax.axis_index("tp")
    dp_at = lax.axis_index("dp")
    core = dp_at % 2

    def swap(value):
        return lax.ppermute(value, "tp", [(0, 1), (1, 0)])

    def across(value, bit):
        return lax.ppermute(value, "dp", [(at, at ^ bit) for at in range(dp_size)])

    def fetch(weight):
        half = weight.shape[0] // 2
        mine = lax.dynamic_slice_in_dim(weight, core * half, half, 0).astype(F32)
        near = swap(mine)
        return near, across(near, 1)

    def row(value):
        return value.reshape(1, -1)

    padded = count // group_sizes[0]
    info = jnp.concatenate(
        [jnp.stack([padded, tp_at.astype(jnp.int32), core.astype(jnp.int32)]), seq_lengths[0]]
    )
    position = (jnp.arange(count, dtype=jnp.int32) % padded).astype(F32)
    halfway = HEAD_DIM // 2
    frequency = jnp.exp(-math.log(10000.0) * jnp.arange(halfway, dtype=F32) / halfway)
    angles = position[:, None] * jnp.tile(frequency, LANES // halfway)[None, :]
    cosine = jnp.cos(angles)
    sine = jnp.sin(angles)

    so_near, so_far = fetch(self_out_w)
    co_near, co_far = fetch(cross_out_w)
    cq_near, cq_far = fetch(cross_q_w)

    qkv_w = jnp.swapaxes(self_qkv_w, 0, 1)
    ln_one, qkv, self_mix, self_lse, mask = call(
        partial(self_forward, slots),
        "self_forward",
        (info,),
        (tokens, qkv_w, self_qkv_b, norm_gain[0:1], norm_bias[0:1], cosine, sine),
        (
            shape((count, width), BF16),
            shape((3 * pairs, count, LANES), BF16),
            shape((count, local)),
            shape((count, LANES)),
            shape((count, count)),
        ),
    )
    self_mix_peer = swap(self_mix)

    kv_w = jnp.swapaxes(cross_kv_w, 0, 1).reshape(2, width, local)
    flat_store = neighbours.reshape(stored * span, width)
    kv_bias = jnp.concatenate([jnp.zeros_like(cross_v_b), cross_v_b])
    joined_kv = jnp.concatenate([kv_w[0], kv_w[1]], axis=1)
    store_kv = (dot(flat_store, joined_kv) + kv_bias).astype(BF16)

    hidden_one, ln_two, cross_query, cross_mix, cross_lse = call(
        partial(cross_forward, slots, span),
        "cross_forward",
        (info, stretch_neighbours),
        (
            tokens,
            self_mix,
            self_mix_peer,
            self_out_w,
            so_near,
            so_far,
            row(self_out_b),
            norm_gain[1:2],
            norm_bias[1:2],
            cross_q_w,
            row(cross_q_b),
            store_kv,
        ),
        (
            shape((count, width)),
            shape((count, width), BF16),
            shape((count, local), BF16),
            shape((count, local)),
            shape((count, LANES)),
        ),
        [pltpu.VMEM((local, width), BF16), pltpu.VMEM((count, local), F32)],
    )
    cross_mix_peer = swap(cross_mix)

    step = 256
    rows = lambda wide: pl.BlockSpec((step, wide), lambda i: (i, 0))
    kept = pl.BlockSpec(memory_space=pltpu.VMEM)
    own_width = width // 2
    hidden_two, ln_three, act, grad_pre, out_keep, out_send, part_three, mlp_in_b_grad = pl.pallas_call(
        feed_forward,
        name="feed_forward",
        grid=(count // step,),
        in_specs=[pl.BlockSpec(memory_space=pltpu.SMEM), rows(width), rows(local), rows(local)]
        + [kept] * 10
        + [rows(width)],
        out_specs=[
            rows(width),
            rows(width),
            rows(hidden),
            rows(hidden),
            rows(own_width),
            rows(own_width),
            rows(width),
            pl.BlockSpec((1, hidden), lambda i: (0, 0)),
        ],
        out_shape=[
            shape((count, width)),
            shape((count, width), BF16),
            shape((count, hidden), BF16),
            shape((count, hidden), BF16),
            shape((count, own_width)),
            shape((count, own_width)),
            shape((count, width)),
            shape((1, hidden)),
        ],
        scratch_shapes=[pltpu.VMEM((local, width), BF16)],
    )(
        info,
        hidden_one,
        cross_mix,
        cross_mix_peer,
        cross_out_w,
        co_near,
        co_far,
        row(cross_out_b),
        norm_gain[2:3],
        norm_bias[2:3],
        mlp_in_w,
        row(mlp_in_b),
        mlp_out_w,
        row(mlp_out_b),
        out_grad,
    )
    part_three_peer = swap(part_three)
    out_back = swap(out_send)
    output = (out_keep + out_back).astype(BF16)

    mlp_out_w_grad = tdot(out_grad, act)
    mlp_in_w_grad = tdot(ln_three, grad_pre)
    mlp_out_b_grad = jnp.sum(out_grad.astype(F32), axis=0, keepdims=True)

    (
        grad_two,
        grad_cross,
        grad_query,
        grad_query_low,
        grad_store,
        gain_three,
        shift_three,
        cross_out_b_grad,
        cross_q_b_grad,
        cross_v_b_grad,
    ) = call(
        partial(cross_backward, slots, span),
        "cross_backward",
        (info, stretch_neighbours),
        (
            part_three,
            part_three_peer,
            hidden_two,
            out_grad,
            norm_gain[2:3],
            cross_out_w,
            cross_query,
            store_kv,
            cross_lse,
        ),
        (
            shape((count, width)),
            shape((count, width), BF16),
            shape((count, local)),
            shape((count, local), BF16),
            shape((stored * span, 2 * local), BF16),
            shape((1, width)),
            shape((1, width)),
            shape((1, width)),
            shape((1, local)),
            shape((1, local)),
        ),
        [
            pltpu.VMEM((count, local), BF16),
            pltpu.VMEM((count, local), F32),
            pltpu.VMEM((stored * span, 2 * local), F32),
        ],
    )
    grad_query_peer = swap(grad_query)

    own_kv = lax.dynamic_slice_in_dim(joined_kv, tp_at * own_width, own_width, 0)
    peer_kv = lax.dynamic_slice_in_dim(joined_kv, (1 - tp_at) * own_width, own_width, 0)
    store_back = swap(dot_t(grad_store, peer_kv))
    neighbours_grad = (dot_t(grad_store, own_kv) + store_back).astype(BF16)
    cross_out_w_grad = tdot(grad_cross, cross_mix.astype(BF16))
    cross_q_w_grad = tdot(ln_two, grad_query_low)
    cross_kv_w_grad = tdot(flat_store, grad_store)

    grad_attn, grad_qkv, tok_keep, tok_send, sums, self_qkv_b_grad = call(
        self_backward,
        "self_backward",
        (info,),
        (
            grad_query_low,
            grad_query_peer,
            cross_q_w,
            cq_near,
            cq_far,
            hidden_one,
            grad_two,
            norm_gain[1:2],
            self_out_w,
            qkv,
            self_lse,
            mask,
            cosine,
            sine,
            qkv_w,
            tokens,
            norm_gain[0:1],
        ),
        (
            shape((count, width), BF16),
            shape((3 * pairs, count, LANES), BF16),
            shape((count, own_width)),
            shape((count, own_width)),
            shape((8, width)),
            shape((1, 3 * local)),
        ),
        [
            pltpu.VMEM((width, local), BF16),
            pltpu.VMEM((count, width), F32),
            pltpu.VMEM((pairs, count, LANES), BF16),
            pltpu.VMEM((count, LANES), F32),
            pltpu.VMEM((count, LANES), F32),
            pltpu.VMEM((256, width), F32),
        ],
    )
    tokens_grad = (tok_keep + swap(tok_send)).astype(BF16)
    self_out_w_grad = tdot(grad_attn, self_mix.astype(BF16))
    self_qkv_w_grad = jnp.concatenate([tdot(ln_one, grad_qkv[piece]) for piece in range(3 * pairs)], axis=1)

    def scatter(value):
        value = value.reshape(dp_size, width // dp_size, value.shape[1])
        bit = 1
        while bit < dp_size:
            value = value.reshape(-1, 2, *value.shape[1:])
            mine = (dp_at // bit) % 2
            sent = lax.dynamic_index_in_dim(value, 1 - mine, 1, keepdims=False)
            held = lax.dynamic_index_in_dim(value, mine, 1, keepdims=False)
            value = held + across(sent, bit)
            bit *= 2
        return value[0]

    mlp_out_w_grad = scatter(mlp_out_w_grad)
    mlp_in_w_grad = scatter(mlp_in_w_grad)
    cross_out_w_grad = scatter(cross_out_w_grad)
    cross_q_w_grad = scatter(cross_q_w_grad)
    cross_kv_w_grad = scatter(cross_kv_w_grad)
    self_out_w_grad = scatter(self_out_w_grad)
    self_qkv_w_grad = scatter(self_qkv_w_grad)

    def total(value):
        bit = 1
        while bit < dp_size:
            value = value + across(value, bit)
            bit *= 2
        return value

    shared = jnp.concatenate(
        [sums[3:5], 0.5 * sums[0:3], 0.5 * gain_three, 0.5 * shift_three, 0.5 * cross_out_b_grad, 0.5 * mlp_out_b_grad],
        axis=0,
    )
    shared = shared + swap(shared)
    alone = jnp.concatenate(
        [self_qkv_b_grad, cross_q_b_grad, cross_v_b_grad, mlp_in_b_grad], axis=1
    )
    alone_size = alone.shape[1]
    alone_rows = -(-alone_size // width)
    alone = jnp.pad(alone, ((0, 0), (0, alone_rows * width - alone_size))).reshape(alone_rows, width)
    summed = total(jnp.concatenate([shared, alone], axis=0))
    alone = summed[9:].reshape(-1)
    norm_gain_grad = jnp.stack([summed[0], summed[2], summed[5]])
    norm_bias_grad = jnp.stack([summed[1], summed[3], summed[6]])
    return (
        output,
        tokens_grad,
        neighbours_grad.reshape(stored, span, own_width),
        norm_gain_grad,
        norm_bias_grad,
        self_qkv_w_grad.reshape(-1, 3, local),
        alone[: 3 * local].reshape(3, local),
        self_out_w_grad.T,
        summed[4],
        cross_q_w_grad,
        alone[3 * local : 4 * local],
        cross_kv_w_grad.reshape(-1, 2, local),
        alone[4 * local : 5 * local],
        cross_out_w_grad.T,
        summed[7],
        mlp_in_w_grad,
        alone[5 * local : 5 * local + hidden],
        mlp_out_w_grad.T,
        summed[8],
    )


def solution(mesh):
    placed = (
        P("dp", None),
        P("dp", None, None),
        P("dp", None),
        P("dp"),
        P("dp", None),
        P("dp", None),
        P(),
        P(),
        P(None, None, "tp"),
        P(None, "tp"),
        P("tp", None),
        P(),
        P(None, "tp"),
        P("tp"),
        P(None, None, "tp"),
        P("tp"),
        P("tp", None),
        P(),
        P(None, "tp"),
        P("tp"),
        P("tp", None),
        P(),
    )
    return jax.shard_map(
        per_device,
        mesh=mesh,
        in_specs=placed,
        out_specs=(
            P("dp", "tp"),
            P("dp", "tp"),
            P("dp", None, "tp"),
            P(),
            P(),
            P("dp", None, "tp"),
            P(None, "tp"),
            P("tp", "dp"),
            P(),
            P("dp", "tp"),
            P("tp"),
            P("dp", None, "tp"),
            P("tp"),
            P("tp", "dp"),
            P(),
            P("dp", "tp"),
            P("tp"),
            P("tp", "dp"),
            P(),
        ),
        check_vma=False,
    )
```

```python
from functools import partial
import math

import jax
import jax.numpy as jnp
from jax import lax
from jax.experimental import pallas as pl
from jax.experimental.pallas import tpu as pltpu
from jax.sharding import PartitionSpec as P

HEAD_DIM = 64
STRETCH = 64
LANES = 128
F32 = jnp.float32
BF16 = jnp.bfloat16
TILE = 128


def dot(left, right):
    return lax.dot_general(left, right, (((1,), (0,)), ((), ())), preferred_element_type=F32)


def dot_t(left, right):
    return lax.dot_general(left, right, (((1,), (1,)), ((), ())), preferred_element_type=F32)


def tdot(left, right):
    return lax.dot_general(left, right, (((0,), (0,)), ((), ())), preferred_element_type=F32)


def norm_stats(field):
    center = field - jnp.mean(field, axis=-1, keepdims=True)
    spread = jnp.mean(center * center, axis=-1, keepdims=True)
    scale = lax.rsqrt(spread + 1e-05)
    return center * scale, scale


def norm_back(xhat, scale, gain, gradient):
    scaled = gradient * gain
    first = jnp.mean(scaled, axis=-1, keepdims=True)
    second = jnp.mean(scaled * xhat, axis=-1, keepdims=True)
    return scale * (scaled - first - xhat * second)


def lane_ids(rows):
    return lax.broadcasted_iota(jnp.int32, (rows, LANES), 1)


def turn(field, cosine, sine, direction):
    lane = lane_ids(field.shape[0])
    ahead = pltpu.roll(field, LANES - HEAD_DIM // 2, 1)
    behind = pltpu.roll(field, HEAD_DIM // 2, 1)
    crossed = jnp.where((lane & (HEAD_DIM - 1)) < HEAD_DIM // 2, -ahead, behind)
    return field * cosine + crossed * (sine * direction)


def two_heads(field):
    low = lane_ids(field.shape[0]) < HEAD_DIM
    zero = jnp.zeros_like(field)
    return jnp.concatenate([jnp.where(low, field, zero), jnp.where(low, zero, field)], axis=0)


def join_heads(field):
    half = field.shape[0] // 2
    return jnp.where(lane_ids(half) < HEAD_DIM, field[:half], field[half:])


def two_columns(columns, first):
    lane = lane_ids(columns.shape[0])
    parts = [
        jnp.sum(jnp.where(lane == first + head, columns, 0.0), axis=-1, keepdims=True)
        for head in range(2)
    ]
    return jnp.concatenate(parts, axis=0)


def put_columns(columns, values, first):
    half = columns.shape[0]
    lane = lane_ids(half)
    columns = jnp.where(lane == first, values[:half], columns)
    return jnp.where(lane == first + 1, values[half:], columns)


def slot_length(ids, info, slots):
    length = jnp.zeros_like(ids)
    for slot in range(slots):
        length = jnp.where(ids >= slot * info[0], info[3 + slot], length)
    return length


def fill_mask(bias_ref, info, slots):
    count = bias_ref.shape[0]
    padded = info[0]
    for start in range(0, count, TILE):
        shape = (TILE, start + TILE)
        rows = lax.broadcasted_iota(jnp.int32, shape, 0) + start
        keys = lax.broadcasted_iota(jnp.int32, shape, 1)
        place = keys & (padded - 1)
        allowed = (
            (keys <= rows)
            & (keys >= rows - (rows & (padded - 1)))
            & (place < slot_length(keys, info, slots))
        )
        bias_ref[start : start + TILE, : start + TILE] = jnp.where(allowed, 0.0, -1e30)


def valid_rows(count, info, slots):
    rows = lax.broadcasted_iota(jnp.int32, (count, LANES), 0)
    shifted = (rows & (info[0] - 1)) + (STRETCH - 1)
    return (shifted < info[0]) & (shifted < slot_length(rows, info, slots))


def join_peer(peer_ref, near_ref, far_ref, core):
    half = peer_ref.shape[0] // 2
    peer_ref[pl.ds(pl.multiple_of(core * half, 64), half), :] = near_ref[...].astype(BF16)
    peer_ref[pl.ds(pl.multiple_of((1 - core) * half, 64), half), :] = far_ref[...].astype(BF16)


def self_forward(slots, info, tok, weight, bias, gains, shifts, cosine, sine, ln_out, qkv_out, mix_out, lse_out, mask_out):
    count = tok.shape[0]
    pairs = weight.shape[2] // LANES
    gain, shift = gains[0:1, :], shifts[0:1, :]
    fill_mask(mask_out, info, slots)
    step = 256

    def project(index, carry):
        rows = pl.ds(pl.multiple_of(index * step, step), step)
        xhat, _ = norm_stats(tok[rows, :].astype(F32))
        ln = (xhat * gain + shift).astype(BF16)
        ln_out[rows, :] = ln
        for part in range(3):
            made = dot(ln, weight[part]) + bias[part : part + 1, :]
            for pair in range(pairs):
                piece = made[:, pair * LANES : (pair + 1) * LANES]
                if part < 2:
                    piece = turn(piece, cosine[rows, :], sine[rows, :], 1.0)
                qkv_out[part * pairs + pair, rows, :] = piece.astype(BF16)
        return carry

    lax.fori_loop(0, count // step, project, 0)

    def attend(pair, carry):
        columns = pl.ds(pl.multiple_of(pair * LANES, LANES), LANES)
        for start in range(0, count, TILE):
            rows = slice(start, start + TILE)
            span = slice(0, start + TILE)
            query = two_heads(qkv_out[pair, rows, :] * BF16(0.125))
            scores = dot_t(query, qkv_out[pairs + pair, span, :])
            mask = mask_out[rows, span]
            scores = scores + jnp.concatenate([mask, mask], axis=0)
            top = jnp.max(scores, axis=-1, keepdims=True)
            expo = jnp.exp(scores - top)
            total = jnp.sum(expo, axis=-1, keepdims=True)
            probs = (expo * (1.0 / total)).astype(BF16)
            mixed = join_heads(dot(probs, qkv_out[2 * pairs + pair, span, :]))
            mix_out[rows, columns] = mixed.astype(BF16).astype(F32)
            lse_out[rows, :] = put_columns(lse_out[rows, :], top + jnp.log(total), 2 * pair)
        return carry

    lax.fori_loop(0, pairs, attend, 0)


def cross_forward(
    slots, span, info, picks, tok, mix_own, mix_peer, w_own, w_near, w_far, out_bias, gains, shifts, q_w, q_b, kv,
    hidden_out, ln_out, query_out, mix_out, lse_out, w_peer, field,
):
    count = tok.shape[0]
    local = q_w.shape[1]
    pairs = local // LANES
    gain, shift = gains[1:2, :], shifts[1:2, :]
    join_peer(w_peer, w_near, w_far, info[2])
    step = 256

    def project(index, carry):
        rows = pl.ds(pl.multiple_of(index * step, step), step)
        attn = dot(mix_own[rows, :].astype(BF16), w_own[...]) + dot(
            mix_peer[rows, :].astype(BF16), w_peer[...]
        )
        hidden = tok[rows, :].astype(F32) + (attn + out_bias[...])
        hidden_out[rows, :] = hidden
        xhat, _ = norm_stats(hidden)
        ln = (xhat * gain + shift).astype(BF16)
        ln_out[rows, :] = ln
        field[rows, :] = dot(ln, q_w[...]) + q_b[...]
        return carry

    lax.fori_loop(0, count // step, project, 0)
    for pair in range(pairs):
        columns = slice(pair * LANES, (pair + 1) * LANES)
        query_out[:, columns] = pltpu.roll(field[:, columns], count - (STRETCH - 1), 0).astype(BF16)

    def block(index, carry):
        rows = pl.ds(pl.multiple_of(index * STRETCH, STRETCH), STRETCH)
        near = pl.ds(pl.multiple_of(picks[index, 0] * span, span), span)
        far = pl.ds(pl.multiple_of(picks[index, 1] * span, span), span)
        lse = jnp.zeros((STRETCH, LANES), F32)
        for pair in range(pairs):
            columns = slice(pair * LANES, (pair + 1) * LANES)
            values = slice(local + pair * LANES, local + (pair + 1) * LANES)
            query = two_heads(query_out[rows, columns] * BF16(0.125))
            keys = jnp.concatenate([kv[near, columns], kv[far, columns]], axis=0)
            vals = jnp.concatenate([kv[near, values], kv[far, values]], axis=0)
            scores = dot_t(query, keys)
            top = jnp.max(scores, axis=-1, keepdims=True)
            expo = jnp.exp(scores - top)
            total = jnp.sum(expo, axis=-1, keepdims=True)
            probs = (expo * (1.0 / total)).astype(BF16)
            field[rows, columns] = join_heads(dot(probs, vals))
            lse = put_columns(lse, top + jnp.log(total), 2 * pair)
        lse_out[rows, :] = lse
        return carry

    lax.fori_loop(0, picks.shape[0], block, 0)
    valid = valid_rows(count, info, slots)
    for pair in range(pairs):
        columns = slice(pair * LANES, (pair + 1) * LANES)
        kept = jnp.where(valid, field[:, columns], 0.0)
        mix_out[:, columns] = pltpu.roll(kept, STRETCH - 1, 0).astype(BF16).astype(F32)


def gelu_parts(field):
    upper = 0.5 * (1.0 + lax.erf(field * (1.0 / math.sqrt(2.0))))
    density = jnp.exp(field * field * -0.5) * (1.0 / math.sqrt(2.0 * math.pi))
    return field * upper, upper + field * density


def feed_forward(
    info, hidden_one, mix_own, mix_peer, w_own, w_near, w_far, out_bias, gains, shifts, in_w, in_b, out_w, end_bias, grad,
    hidden_out, ln_out, act_out, pre_out, keep_out, send_out, part_out, bias_out, w_peer,
):
    @pl.when(pl.program_id(0) == 0)
    def _():
        join_peer(w_peer, w_near, w_far, info[2])
        bias_out[...] = jnp.zeros_like(bias_out)

    half = keep_out.shape[1]
    own = pl.ds(pl.multiple_of(info[1] * half, LANES), half)
    peer = pl.ds(pl.multiple_of((1 - info[1]) * half, LANES), half)
    cross = dot(mix_own[...].astype(BF16), w_own[...]) + dot(mix_peer[...].astype(BF16), w_peer[...])
    hidden = hidden_one[...] + (cross + out_bias[...])
    hidden_out[...] = hidden
    xhat, _ = norm_stats(hidden)
    ln = (xhat * gains[2:3, :] + shifts[2:3, :]).astype(BF16)
    ln_out[...] = ln
    act, slope = gelu_parts(dot(ln, in_w[...]) + in_b[...])
    act = act.astype(BF16)
    act_out[...] = act
    grad_pre = (dot_t(grad[...], out_w[...]) * slope).astype(BF16)
    pre_out[...] = grad_pre
    bias_out[...] += jnp.sum(grad_pre.astype(F32), axis=0, keepdims=True)
    part_out[...] = dot_t(grad_pre, in_w[...])
    keep_out[...] = dot(act, out_w[:, own]) + (hidden_out[:, own] + end_bias[:, own])
    send_out[...] = dot(act, out_w[:, peer])


def cross_backward(
    slots, span, order, info, picks, part_own, part_peer, hidden, out_grad, gains, out_w, query, kv, lse,
    mix, ln, flat_store,
    grad_out, query_out, query_low, store_out, sums_out, q_bias_out, v_bias_out, keep_out, send_one, send_two,
    rows_grad, field, store, low_out, turned, ordered,
):
    count = hidden.shape[0]
    local = query.shape[1]
    pairs = local // LANES
    step = 256
    gain = gains[2:3, :]
    sums_out[...] = jnp.zeros_like(sums_out)
    store[...] = jnp.zeros_like(store)

    def project(index, carry):
        rows = pl.ds(pl.multiple_of(index * step, step), step)
        gradient = part_own[rows, :] + part_peer[rows, :]
        xhat, scale = norm_stats(hidden[rows, :])
        sums_out[0:1, :] += jnp.sum(gradient * xhat, axis=0, keepdims=True)
        sums_out[1:2, :] += jnp.sum(gradient, axis=0, keepdims=True)
        cotangent = out_grad[rows, :].astype(F32)
        sums_out[3:4, :] += jnp.sum(cotangent, axis=0, keepdims=True)
        two = cotangent + norm_back(xhat, scale, gain, gradient)
        grad_out[rows, :] = two
        low = two.astype(BF16)
        low_out[rows, :] = low
        sums_out[2:3, :] += jnp.sum(low.astype(F32), axis=0, keepdims=True)
        field[rows, :] = dot_t(low, out_w[...])
        return carry

    lax.fori_loop(0, count // step, project, 0)
    valid = valid_rows(count, info, slots)
    for pair in range(pairs):
        columns = slice(pair * LANES, (pair + 1) * LANES)
        moved = pltpu.roll(field[:, columns].astype(BF16).astype(F32), count - (STRETCH - 1), 0)
        rows_grad[:, columns] = jnp.where(valid, moved, 0.0).astype(BF16)

    def block(index, carry):
        rows = pl.ds(pl.multiple_of(index * STRETCH, STRETCH), STRETCH)
        near = pl.ds(pl.multiple_of(picks[index, 0] * span, span), span)
        far = pl.ds(pl.multiple_of(picks[index, 1] * span, span), span)
        logs = lse[rows, :]
        for pair in range(pairs):
            columns = slice(pair * LANES, (pair + 1) * LANES)
            values = slice(local + pair * LANES, local + (pair + 1) * LANES)
            query_two = two_heads(query[rows, columns] * BF16(0.125))
            grad_two = two_heads(rows_grad[rows, columns])
            keys = jnp.concatenate([kv[near, columns], kv[far, columns]], axis=0)
            vals = jnp.concatenate([kv[near, values], kv[far, values]], axis=0)
            probs = jnp.exp(dot_t(query_two, keys) - two_columns(logs, 2 * pair))
            grad_probs = dot_t(grad_two, vals)
            delta = jnp.sum(probs * grad_probs, axis=-1, keepdims=True)
            grad_scores = (probs * (grad_probs - delta)).astype(BF16)
            field[rows, columns] = join_heads(dot(grad_scores, keys)) * 0.125
            grad_keys = tdot(grad_scores, query_two)
            grad_vals = tdot(probs.astype(BF16), grad_two)
            store[near, columns] += grad_keys[:span]
            store[far, columns] += grad_keys[span:]
            store[near, values] += grad_vals[:span]
            store[far, values] += grad_vals[span:]
        return carry

    lax.fori_loop(0, picks.shape[0], block, 0)
    for pair in range(pairs):
        columns = slice(pair * LANES, (pair + 1) * LANES)
        low = pltpu.roll(field[:, columns], STRETCH - 1, 0).astype(BF16)
        query_low[:, columns] = low
        query_out[:, columns] = low.astype(F32)
        q_bias_out[:, columns] = jnp.sum(low.astype(F32), axis=0, keepdims=True)

    v_bias_out[...] = jnp.zeros_like(v_bias_out)

    def flush(index, carry):
        rows = pl.ds(pl.multiple_of(index * span, span), span)
        low = store[rows, :].astype(BF16)
        store_out[rows, :] = low
        v_bias_out[...] += jnp.sum(low[:, local:].astype(F32), axis=0, keepdims=True)
        return carry

    lax.fori_loop(0, store.shape[0] // span, flush, 0)
    terms = ((low_out, mix), (ln, query_low), (flat_store, store_out))
    fill_grads(order, info[3 + slots], terms, keep_out, (send_one, send_two), turned, ordered)


def self_backward(
    slots, order, info, query_own, query_peer, q_w, q_near, q_far, hidden, grad_two, gains, out_w, qkv, lse, mask, cosine, sine, w,
    tok, cross_sums, q_bias, v_bias, in_bias, out_send, mix, ln,
    keep_out, send_out, sums_out, grads_keep, grads_one, grads_two,
    q_peer, one, mix_grad, key_grad, value_grad, part, low_out, qkv_out, turned, ordered,
):
    count = tok.shape[0]
    local = out_w.shape[0]
    pairs = local // LANES
    step = 256
    gain_one, gain_two = gains[0:1, :], gains[1:2, :]
    join_peer(q_peer, q_near, q_far, info[2])
    sums_out[...] = jnp.zeros_like(sums_out)
    half = keep_out.shape[1]
    own = pl.ds(pl.multiple_of(info[1] * half, LANES), half)
    peer = pl.ds(pl.multiple_of((1 - info[1]) * half, LANES), half)

    def project(index, carry):
        rows = pl.ds(pl.multiple_of(index * step, step), step)
        gradient = dot_t(query_own[rows, :], q_w[...]) + dot(
            query_peer[rows, :].astype(BF16), q_peer[...]
        )
        xhat, scale = norm_stats(hidden[rows, :])
        sums_out[2:3, :] += jnp.sum(gradient * xhat, axis=0, keepdims=True)
        sums_out[3:4, :] += jnp.sum(gradient, axis=0, keepdims=True)
        grad_one = grad_two[rows, :] + norm_back(xhat, scale, gain_two, gradient)
        one[rows, :] = grad_one
        low = grad_one.astype(BF16)
        low_out[rows, :] = low
        sums_out[4:5, :] += jnp.sum(low.astype(F32), axis=0, keepdims=True)
        mixed = dot_t(low, out_w[...])
        for pair in range(pairs):
            mix_grad[pair, rows, :] = mixed[:, pair * LANES : (pair + 1) * LANES].astype(BF16)
        return carry

    lax.fori_loop(0, count // step, project, 0)

    def attend(pair, carry):
        key_grad[...] = jnp.zeros_like(key_grad)
        value_grad[...] = jnp.zeros_like(value_grad)
        for start in range(0, count, TILE):
            rows = slice(start, start + TILE)
            until = slice(0, start + TILE)
            query = two_heads(qkv[pair, rows, :] * BF16(0.125))
            keys = qkv[pairs + pair, until, :]
            vals = qkv[2 * pairs + pair, until, :]
            grad_mix = two_heads(mix_grad[pair, rows, :])
            allowed = mask[rows, until]
            scores = dot_t(query, keys) + jnp.concatenate([allowed, allowed], axis=0)
            probs = jnp.exp(scores - two_columns(lse[rows, :], 2 * pair))
            grad_probs = dot_t(grad_mix, vals)
            delta = jnp.sum(probs * grad_probs, axis=-1, keepdims=True)
            grad_scores = (probs * (grad_probs - delta)).astype(BF16)
            grad_query = join_heads(dot(grad_scores, keys)) * 0.125
            back = turn(grad_query, cosine[rows, :], sine[rows, :], -1.0)
            qkv_out[pair, rows, :] = back.astype(BF16)
            key_grad[until, :] += tdot(grad_scores, query)
            value_grad[until, :] += tdot(probs.astype(BF16), grad_mix)
        for start in range(0, count, TILE):
            rows = slice(start, start + TILE)
            back = turn(key_grad[rows, :], cosine[rows, :], sine[rows, :], -1.0)
            qkv_out[pairs + pair, rows, :] = back.astype(BF16)
            qkv_out[2 * pairs + pair, rows, :] = value_grad[rows, :].astype(BF16)
        return carry

    lax.fori_loop(0, pairs, attend, 0)

    sums_out[5:9, :] = cross_sums[0:4, :]

    def place(piece, columns):
        start = (piece % 2) * local
        sums_out[9 + piece // 2 : 10 + piece // 2, start : start + local] = columns

    for part_at in range(3):
        place(
            part_at,
            jnp.concatenate(
                [
                    jnp.sum(qkv_out[part_at * pairs + pair].astype(F32), axis=0, keepdims=True)
                    for pair in range(pairs)
                ],
                axis=1,
            ),
        )
    place(3, q_bias[...])
    place(4, v_bias[...])
    for piece in range(in_bias.shape[1] // local):
        place(5 + piece, in_bias[:, piece * local : (piece + 1) * local])

    def finish(index, carry):
        rows = pl.ds(pl.multiple_of(index * step, step), step)
        gradient = jnp.zeros((step, tok.shape[1]), F32)
        for part_at in range(3):
            joined = jnp.concatenate(
                [qkv_out[part_at * pairs + pair, rows, :] for pair in range(pairs)], axis=1
            )
            gradient = gradient + dot_t(joined, w[part_at])
        xhat, scale = norm_stats(tok[rows, :].astype(F32))
        sums_out[0:1, :] += jnp.sum(gradient * xhat, axis=0, keepdims=True)
        sums_out[1:2, :] += jnp.sum(gradient, axis=0, keepdims=True)
        part[...] = norm_back(xhat, scale, gain_one, gradient)
        keep_out[rows, :] = part[:, own] + one[rows, own]
        send_out[rows, :half] = part[:, peer]
        send_out[rows, half:] = out_send[rows, :]
        return carry

    lax.fori_loop(0, count // step, finish, 0)
    terms = ((low_out, mix), (ln, qkv_out))
    fill_grads(order, info[3 + slots], terms, grads_keep, (grads_one, grads_two), turned, ordered)


def slice_at(place, order):
    last = len(order) - 1
    return sum(bit * ((place >> (last - at)) & 1) for at, bit in enumerate(order))


def fill_grads(order, me, terms, keep_out, send_outs, turned, ordered):
    width = turned.shape[0]
    half = width // 2
    share = send_outs[0].shape[1]
    column = 0
    for left, right in terms:
        count = left.shape[0]
        if order is None:
            ordered[:, :count] = left[...].T
        else:
            parts = 1 << len(order)
            slab = width // parts
            turned[:, :count] = left[...].T

            def move(place, carry, count=count):
                source = pl.multiple_of((me ^ slice_at(place, order)) * slab, 16)
                target = pl.multiple_of(place * slab, 16)
                ordered[pl.ds(target, slab), :count] = turned[pl.ds(source, slab), :count]
                return carry

            lax.fori_loop(0, parts, move, 0)
        pieces = right.shape[0] if len(right.shape) == 3 else right.shape[1] // LANES
        group = 3
        wide = group * LANES
        for index in range(pieces // group):
            if len(right.shape) == 3:
                field = jnp.concatenate([right[index * group + at] for at in range(group)], axis=1)
            else:
                field = right[:, index * wide : (index + 1) * wide]
            field = field.astype(BF16)
            keep_out[:, column : column + wide] = dot(ordered[:half, :count], field)
            at = column % share
            send_outs[column // share][:, at : at + wide] = dot(ordered[half:, :count], field)
            column += wide


def weight_grads(order, me_at, info, *refs):
    products = (len(refs) - 7) // 2
    lefts, rights = refs[:products], refs[products : 2 * products]
    keep_out, *send_outs = refs[2 * products : -2]
    fill_grads(order, info[me_at], zip(lefts, rights), keep_out, send_outs, *refs[-2:])


def add_halves(pieces, joined, split, *refs):
    kept, came = refs[:2], refs[2 : 2 + 2 * pieces]
    outs = refs[2 + 2 * pieces + (2 if joined else 0) :]
    share = came[0].shape[1]
    for side in range(2):
        for piece in range(pieces):
            start = piece * share
            value = kept[side][:, start : start + share] + came[2 * piece + side][...]
            if start < split:
                outs[side][:, start : start + share] = value
            else:
                outs[2 + side][:, start - split : start - split + share] = value
        if joined:
            outs[side][:, pieces * share :] = refs[2 + 2 * pieces + side][...]


def whole(count):
    return [pl.BlockSpec(memory_space=pltpu.VMEM)] * count


def scalars(count):
    return [pl.BlockSpec(memory_space=pltpu.SMEM)] * count


def shape(dims, kind=F32):
    return jax.ShapeDtypeStruct(dims, kind)


def after(value, *others):
    return lax.optimization_barrier((value, *others))[0]


def work(flops):
    return pl.CostEstimate(flops=flops, bytes_accessed=1, transcendentals=0)


def call(body, name, small, big, outs, scratch=(), flops=0):
    return pl.pallas_call(
        body,
        name=name,
        out_shape=outs,
        in_specs=scalars(len(small)) + whole(len(big)),
        out_specs=whole(len(outs)),
        scratch_shapes=scratch,
        cost_estimate=work(flops),
    )(*small, *big)


def per_device(
    tokens,
    neighbours,
    out_grad,
    group_sizes,
    seq_lengths,
    stretch_neighbours,
    norm_gain,
    norm_bias,
    self_qkv_w,
    self_qkv_b,
    self_out_w,
    self_out_b,
    cross_q_w,
    cross_q_b,
    cross_kv_w,
    cross_v_b,
    cross_out_w,
    cross_out_b,
    mlp_in_w,
    mlp_in_b,
    mlp_out_w,
    mlp_out_b,
):
    count, width = tokens.shape
    local = self_qkv_w.shape[2]
    hidden = mlp_in_w.shape[1]
    pairs = local // LANES
    stored, span = neighbours.shape[:2]
    slots = seq_lengths.shape[1]
    dp_size = lax.axis_size("dp")
    slab = width // dp_size
    tp_at = lax.axis_index("tp")
    dp_at = lax.axis_index("dp")
    core = dp_at % 2

    def swap(value):
        return lax.ppermute(value, "tp", [(0, 1), (1, 0)])

    def across(value, bit):
        return lax.ppermute(value, "dp", [(at, at ^ bit) for at in range(dp_size)])

    def mine(weight):
        half = weight.shape[0] // 2
        return lax.dynamic_slice_in_dim(weight, core * half, half, 0).astype(F32)

    def mine_turned(weight):
        half = weight.shape[1] // 2
        return lax.dynamic_slice_in_dim(weight, core * half, half, 1).T.astype(F32)

    def row(value):
        return value.reshape(1, -1)

    padded = count // group_sizes[0]
    info = jnp.concatenate(
        [
            jnp.stack([padded, tp_at.astype(jnp.int32), core.astype(jnp.int32)]),
            seq_lengths[0],
            dp_at.astype(jnp.int32)[None],
        ]
    )
    position = (jnp.arange(count, dtype=jnp.int32) % padded).astype(F32)
    halfway = HEAD_DIM // 2
    frequency = jnp.exp(-math.log(10000.0) * jnp.arange(halfway, dtype=F32) / halfway)
    angles = position[:, None] * jnp.tile(frequency, LANES // halfway)[None, :]
    cosine = jnp.cos(angles)
    sine = jnp.sin(angles)

    bits = [1 << at for at in range(dp_size.bit_length() - 1)]
    order = bits if slab % 16 == 0 else None

    def add_sent(name, kept, came, joined=(), split=None):
        rows, total = kept.shape[0] // 2, kept.shape[1]
        split = split or total
        steps = 4
        block = rows // steps

        def sides(value):
            wide = value.shape[1]
            return [
                pl.BlockSpec((block, wide), lambda i: (i, 0)),
                pl.BlockSpec((block, wide), lambda i: (i + steps, 0)),
            ]

        straight = lambda wide: pl.BlockSpec((block, wide), lambda i: (i, 0))
        first = split + sum(value.shape[1] for value in joined[:1])
        wides = [first, first] + ([total - split] * 2 if split < total else [])
        return pl.pallas_call(
            partial(add_halves, len(came), bool(joined), split),
            name=name,
            grid=(steps,),
            in_specs=[spec for value in (kept, *came) for spec in sides(value)]
            + [straight(value.shape[1]) for value in joined],
            out_specs=[straight(wide) for wide in wides],
            out_shape=[shape((rows, wide)) for wide in wides],
            cost_estimate=work(0),
        )(*[value for value in (kept, *came) for _ in range(2)], *joined)

    def sorted_halves(kept, *sent):
        if order is not None:
            return kept, sent
        value = jnp.concatenate([kept, jnp.concatenate(sent, axis=1)], axis=0)
        places = jnp.array([slice_at(place, bits) for place in range(dp_size)], jnp.int32) ^ dp_at
        value = jnp.take(value.reshape(dp_size, slab, -1), places, axis=0).reshape(value.shape)
        return value[: width // 2], jnp.split(value[width // 2 :], len(sent), axis=1)

    def core_halve(halves, gate=None):
        kept, sent = halves
        came = jnp.concatenate([across(piece, 1) for piece in sent], axis=1)
        return merge(kept if gate is None else after(kept, *gate), came)

    def grads_of(total, shares):
        return (shape((width // 2, total)),) + (shape((width // 2, total // shares)),) * shares

    def turning(most):
        return [pltpu.VMEM((width, most), BF16), pltpu.VMEM((width, most), BF16)]

    def merge(kept, arrived):
        half = kept.shape[0] // 2
        return kept[:half] + arrived[:half], kept[half:] + arrived[half:]

    def halve(kept, sent, bit):
        return merge(kept, across(sent, bit))

    so_near = swap(mine(self_out_w))
    qkv_w = jnp.swapaxes(self_qkv_w, 0, 1)
    ln_one, qkv, self_mix, self_lse, mask = call(
        partial(self_forward, slots),
        "self_forward",
        (info,),
        (tokens, qkv_w, self_qkv_b, norm_gain, norm_bias, cosine, sine),
        (
            shape((count, width), BF16),
            shape((3 * pairs, count, LANES), BF16),
            shape((count, local)),
            shape((count, LANES)),
            shape((count, count)),
        ),
        flops=11_000_000_000,
    )
    self_mix_peer = swap(self_mix)
    so_far = across(so_near, 1)

    kv_w = jnp.swapaxes(cross_kv_w, 0, 1).reshape(2, width, local)
    flat_store = neighbours.reshape(stored * span, width)
    kv_bias = jnp.concatenate([jnp.zeros_like(cross_v_b), cross_v_b])
    joined_kv = jnp.concatenate([kv_w[0], kv_w[1]], axis=1)
    store_kv = (dot(flat_store, joined_kv) + kv_bias).astype(BF16)

    co_near = swap(after(mine(cross_out_w), self_mix_peer))
    hidden_one, ln_two, cross_query, cross_mix, cross_lse = call(
        partial(cross_forward, slots, span),
        "cross_forward",
        (info, stretch_neighbours),
        (
            tokens,
            self_mix,
            self_mix_peer,
            self_out_w,
            so_near,
            so_far,
            row(self_out_b),
            norm_gain,
            norm_bias,
            cross_q_w,
            row(cross_q_b),
            store_kv,
        ),
        (
            shape((count, width)),
            shape((count, width), BF16),
            shape((count, local), BF16),
            shape((count, local)),
            shape((count, LANES)),
        ),
        [pltpu.VMEM((local, width), BF16), pltpu.VMEM((count, local), F32)],
        flops=14_000_000_000,
    )
    cross_mix_peer = swap(cross_mix)
    co_far = across(co_near, 1)
    cq_near = swap(after(mine_turned(cross_q_w), cross_mix_peer))

    step = 256
    rows = lambda wide: pl.BlockSpec((step, wide), lambda i: (i, 0))
    kept = pl.BlockSpec(memory_space=pltpu.VMEM)
    own_width = width // 2
    hidden_two, ln_three, act, grad_pre, out_keep, out_send, part_three, mlp_in_b_grad = pl.pallas_call(
        feed_forward,
        name="feed_forward",
        grid=(count // step,),
        in_specs=[pl.BlockSpec(memory_space=pltpu.SMEM), rows(width), rows(local), rows(local)]
        + [kept] * 10
        + [rows(width)],
        out_specs=[
            rows(width),
            rows(width),
            rows(hidden),
            rows(hidden),
            rows(own_width),
            rows(own_width),
            rows(width),
            pl.BlockSpec((1, hidden), lambda i: (0, 0)),
        ],
        out_shape=[
            shape((count, width)),
            shape((count, width), BF16),
            shape((count, hidden), BF16),
            shape((count, hidden), BF16),
            shape((count, own_width)),
            shape((count, own_width)),
            shape((count, width)),
            shape((1, hidden)),
        ],
        scratch_shapes=[pltpu.VMEM((local, width), BF16)],
        cost_estimate=work(14_000_000_000),
    )(
        info,
        hidden_one,
        cross_mix,
        cross_mix_peer,
        cross_out_w,
        co_near,
        co_far,
        row(cross_out_b),
        norm_gain,
        norm_bias,
        mlp_in_w,
        row(mlp_in_b),
        mlp_out_w,
        row(mlp_out_b),
        out_grad,
    )
    part_three_peer = swap(part_three)
    cq_far = across(cq_near, 1)
    mlp = sorted_halves(
        *call(
            partial(weight_grads, order, 3 + slots),
            "mlp_grads",
            (info,),
            (after(out_grad, cq_near), ln_three, act, grad_pre),
            grads_of(2 * hidden, 4),
            turning(count),
            flops=0,
        )
    )
    came_mlp = [across(piece, 1) for piece in mlp[1]]
    *first, late_kept, late_sent = add_sent("add_mlp", mlp[0], came_mlp, split=3 * hidden // 2)
    (
        grad_two,
        grad_query,
        grad_query_low,
        grad_store,
        cross_sums,
        cross_q_b_grad,
        cross_v_b_grad,
        *cross_halves,
    ) = call(
        partial(cross_backward, slots, span, order),
        "cross_backward",
        (info, stretch_neighbours),
        (
            part_three,
            part_three_peer,
            after(hidden_two, first[1]),
            out_grad,
            norm_gain,
            cross_out_w,
            cross_query,
            store_kv,
            cross_lse,
            cross_mix,
            ln_two,
            flat_store,
        ),
        (
            shape((count, width)),
            shape((count, local)),
            shape((count, local), BF16),
            shape((stored * span, 2 * local), BF16),
            shape((8, width)),
            shape((1, local)),
            shape((1, local)),
            *grads_of(4 * local, 2),
        ),
        [
            pltpu.VMEM((count, local), BF16),
            pltpu.VMEM((count, local), F32),
            pltpu.VMEM((stored * span, 2 * local), F32),
            pltpu.VMEM((count, width), BF16),
            *turning(max(count, stored * span)),
        ],
        flops=17_000_000_000,
    )
    grad_query_peer = swap(grad_query)
    first = halve(*first, bits[1])

    own_kv = lax.dynamic_slice_in_dim(joined_kv, tp_at * own_width, own_width, 0)
    peer_kv = lax.dynamic_slice_in_dim(joined_kv, (1 - tp_at) * own_width, own_width, 0)
    store_send = dot_t(grad_store, peer_kv)
    store_keep = dot_t(grad_store, own_kv)
    cross = sorted_halves(*cross_halves)
    came_cross = [across(piece, 1) for piece in cross[1]]
    third = add_sent("add_cross", cross[0], came_cross, (late_kept, late_sent))
    store_back = swap(after(store_send, third[1]))

    tok_keep, both_send, sums, *self_halves = call(
        partial(self_backward, slots, order),
        "self_backward",
        (info,),
        (
            grad_query_low,
            grad_query_peer,
            cross_q_w,
            cq_near,
            cq_far,
            hidden_one,
            after(grad_two, third[1], first[1]),
            norm_gain,
            self_out_w,
            qkv,
            self_lse,
            mask,
            cosine,
            sine,
            qkv_w,
            tokens,
            cross_sums,
            cross_q_b_grad,
            cross_v_b_grad,
            mlp_in_b_grad,
            out_send,
            self_mix,
            ln_one,
        ),
        (
            shape((count, own_width)),
            shape((count, width)),
            shape((16, width)),
            *grads_of(4 * local, 2),
        ),
        [
            pltpu.VMEM((local, width), BF16),
            pltpu.VMEM((count, width), F32),
            pltpu.VMEM((pairs, count, LANES), BF16),
            pltpu.VMEM((count, LANES), F32),
            pltpu.VMEM((count, LANES), F32),
            pltpu.VMEM((256, width), F32),
            pltpu.VMEM((count, width), BF16),
            pltpu.VMEM((3 * pairs, count, LANES), BF16),
            *turning(count),
        ],
        flops=40_000_000_000,
    )
    back = swap(both_send)
    tokens_grad = (tok_keep + back[:, :own_width]).astype(BF16)
    output = (out_keep + back[:, own_width:]).astype(BF16)
    neighbours_grad = (store_keep + store_back).astype(BF16)

    first_came = across(first[1], bits[2])
    third_came = across(third[1], bits[1])
    fourth = core_halve(sorted_halves(*self_halves), (first_came, third_came, store_back))
    first = merge(first[0], first_came)
    third = merge(third[0], third_came)
    sums, *first = lax.optimization_barrier((sums, *first, fourth[1]))[:3]

    def finish(parts, order):
        for bit in order[:-1]:
            parts = halve(*parts, bit)
        return parts[0] + across(parts[1], order[-1])

    mlp_grads = finish(first, bits[3:])
    third = finish(third, bits[2:])
    self_grads = finish(fourth, bits[1:])
    cross_grads = third[:, : 4 * local]
    mlp_out_w_grad = mlp_grads[:, :hidden]
    mlp_in_w_grad = jnp.concatenate([mlp_grads[:, hidden:], third[:, 4 * local :]], axis=1)

    bit = 1
    while bit < dp_size:
        sums = sums + across(sums, bit)
        bit *= 2
    shared = 0.5 * sums[2:9]
    shared = jnp.concatenate([sums[0:2], shared], axis=0)
    shared = shared + swap(shared)
    alone = sums[9:].reshape(-1)
    return (
        output,
        tokens_grad,
        neighbours_grad.reshape(stored, span, own_width),
        jnp.stack([shared[0], shared[2], shared[5]]),
        jnp.stack([shared[1], shared[3], shared[6]]),
        self_grads[:, local:].reshape(-1, 3, local),
        alone[: 3 * local].reshape(3, local),
        self_grads[:, :local].T,
        shared[4],
        cross_grads[:, local : 2 * local],
        alone[3 * local : 4 * local],
        cross_grads[:, 2 * local :].reshape(-1, 2, local),
        alone[4 * local : 5 * local],
        cross_grads[:, :local].T,
        shared[7],
        mlp_in_w_grad,
        alone[5 * local : 5 * local + hidden],
        mlp_out_w_grad.T,
        shared[8],
    )


def solution(mesh):
    placed = (
        P("dp", None),
        P("dp", None, None),
        P("dp", None),
        P("dp"),
        P("dp", None),
        P("dp", None),
        P(),
        P(),
        P(None, None, "tp"),
        P(None, "tp"),
        P("tp", None),
        P(),
        P(None, "tp"),
        P("tp"),
        P(None, None, "tp"),
        P("tp"),
        P("tp", None),
        P(),
        P(None, "tp"),
        P("tp"),
        P("tp", None),
        P(),
    )
    return jax.shard_map(
        per_device,
        mesh=mesh,
        in_specs=placed,
        out_specs=(
            P("dp", "tp"),
            P("dp", "tp"),
            P("dp", None, "tp"),
            P(),
            P(),
            P("dp", None, "tp"),
            P(None, "tp"),
            P("tp", "dp"),
            P(),
            P("dp", "tp"),
            P("tp"),
            P("dp", None, "tp"),
            P("tp"),
            P("tp", "dp"),
            P(),
            P("dp", "tp"),
            P("tp"),
            P("tp", "dp"),
            P(),
        ),
        check_vma=False,
    )
```

```python
from functools import partial
import math

import jax
import jax.numpy as jnp
from jax import lax
from jax.experimental import pallas as pl
from jax.experimental.pallas import tpu as pltpu
from jax.sharding import PartitionSpec as P

HEAD_DIM = 64
STRETCH = 64
LANES = 128
F32 = jnp.float32
BF16 = jnp.bfloat16
TILE = 128
RIDE = 8


def dot(left, right):
    return lax.dot_general(left, right, (((1,), (0,)), ((), ())), preferred_element_type=F32)


def dot_t(left, right):
    return lax.dot_general(left, right, (((1,), (1,)), ((), ())), preferred_element_type=F32)


def tdot(left, right):
    return lax.dot_general(left, right, (((0,), (0,)), ((), ())), preferred_element_type=F32)


def norm_stats(field):
    center = field - jnp.mean(field, axis=-1, keepdims=True)
    spread = jnp.mean(center * center, axis=-1, keepdims=True)
    scale = lax.rsqrt(spread + 1e-05)
    return center * scale, scale


def norm_back(xhat, scale, gain, gradient):
    scaled = gradient * gain
    first = jnp.mean(scaled, axis=-1, keepdims=True)
    second = jnp.mean(scaled * xhat, axis=-1, keepdims=True)
    return scale * (scaled - first - xhat * second)


def lane_ids(rows):
    return lax.broadcasted_iota(jnp.int32, (rows, LANES), 1)


def turn(field, cosine, sine, direction):
    lane = lane_ids(field.shape[0])
    ahead = pltpu.roll(field, LANES - HEAD_DIM // 2, 1)
    behind = pltpu.roll(field, HEAD_DIM // 2, 1)
    crossed = jnp.where((lane & (HEAD_DIM - 1)) < HEAD_DIM // 2, -ahead, behind)
    return field * cosine + crossed * (sine * direction)


def two_heads(field):
    low = lane_ids(field.shape[0]) < HEAD_DIM
    zero = jnp.zeros_like(field)
    return jnp.concatenate([jnp.where(low, field, zero), jnp.where(low, zero, field)], axis=0)


def join_heads(field):
    half = field.shape[0] // 2
    return jnp.where(lane_ids(half) < HEAD_DIM, field[:half], field[half:])


def two_columns(columns, first):
    lane = lane_ids(columns.shape[0])
    parts = [
        jnp.sum(jnp.where(lane == first + head, columns, 0.0), axis=-1, keepdims=True)
        for head in range(2)
    ]
    return jnp.concatenate(parts, axis=0)


def put_columns(columns, values, first):
    half = columns.shape[0]
    lane = lane_ids(half)
    columns = jnp.where(lane == first, values[:half], columns)
    return jnp.where(lane == first + 1, values[half:], columns)


def slot_length(ids, info, slots):
    length = jnp.zeros_like(ids)
    for slot in range(slots):
        length = jnp.where(ids >= slot * info[0], info[3 + slot], length)
    return length


def fill_mask(bias_ref, info, slots):
    count = bias_ref.shape[0]
    padded = info[0]
    for start in range(0, count, TILE):
        shape = (TILE, start + TILE)
        rows = lax.broadcasted_iota(jnp.int32, shape, 0) + start
        keys = lax.broadcasted_iota(jnp.int32, shape, 1)
        place = keys & (padded - 1)
        allowed = (
            (keys <= rows)
            & (keys >= rows - (rows & (padded - 1)))
            & (place < slot_length(keys, info, slots))
        )
        bias_ref[start : start + TILE, : start + TILE] = jnp.where(allowed, 0.0, -1e30)


def valid_rows(count, info, slots):
    rows = lax.broadcasted_iota(jnp.int32, (count, LANES), 0)
    shifted = (rows & (info[0] - 1)) + (STRETCH - 1)
    return (shifted < info[0]) & (shifted < slot_length(rows, info, slots))


def join_peer(peer_ref, near_ref, far_ref, core):
    half = peer_ref.shape[0] // 2
    peer_ref[pl.ds(pl.multiple_of(core * half, 64), half), :] = near_ref[...].astype(BF16)
    peer_ref[pl.ds(pl.multiple_of((1 - core) * half, 64), half), :] = far_ref[...].astype(BF16)


def self_forward(slots, info, tok, weight, bias, gains, shifts, cosine, sine, ln_out, qkv_out, mix_out, lse_out, mask_out):
    count = tok.shape[0]
    pairs = weight.shape[2] // LANES
    gain, shift = gains[0:1, :], shifts[0:1, :]
    fill_mask(mask_out, info, slots)
    step = 256

    def project(index, carry):
        rows = pl.ds(pl.multiple_of(index * step, step), step)
        xhat, _ = norm_stats(tok[rows, :].astype(F32))
        ln = (xhat * gain + shift).astype(BF16)
        ln_out[rows, :] = ln
        for part in range(3):
            made = dot(ln, weight[part]) + bias[part : part + 1, :]
            for pair in range(pairs):
                piece = made[:, pair * LANES : (pair + 1) * LANES]
                if part < 2:
                    piece = turn(piece, cosine[rows, :], sine[rows, :], 1.0)
                qkv_out[part * pairs + pair, rows, :] = piece.astype(BF16)
        return carry

    lax.fori_loop(0, count // step, project, 0)

    def attend(pair, carry):
        columns = pl.ds(pl.multiple_of(pair * LANES, LANES), LANES)
        for start in range(0, count, TILE):
            rows = slice(start, start + TILE)
            span = slice(0, start + TILE)
            query = two_heads(qkv_out[pair, rows, :] * BF16(0.125))
            scores = dot_t(query, qkv_out[pairs + pair, span, :])
            mask = mask_out[rows, span]
            scores = scores + jnp.concatenate([mask, mask], axis=0)
            top = jnp.max(scores, axis=-1, keepdims=True)
            expo = jnp.exp(scores - top)
            total = jnp.sum(expo, axis=-1, keepdims=True)
            probs = (expo * (1.0 / total)).astype(BF16)
            mixed = join_heads(dot(probs, qkv_out[2 * pairs + pair, span, :]))
            mix_out[rows, columns] = mixed.astype(BF16).astype(F32)
            lse_out[rows, :] = put_columns(lse_out[rows, :], top + jnp.log(total), 2 * pair)
        return carry

    lax.fori_loop(0, pairs, attend, 0)


def cross_forward(
    slots, span, info, picks, tok, mix_own, mix_peer, w_own, w_near, w_far, out_bias, gains, shifts, q_w, q_b, kv,
    hidden_out, ln_out, query_out, mix_out, lse_out, w_peer, field,
):
    count = tok.shape[0]
    local = q_w.shape[1]
    pairs = local // LANES
    gain, shift = gains[1:2, :], shifts[1:2, :]
    join_peer(w_peer, w_near, w_far, info[2])
    step = 256

    def project(index, carry):
        rows = pl.ds(pl.multiple_of(index * step, step), step)
        attn = dot(mix_own[rows, :].astype(BF16), w_own[...]) + dot(
            mix_peer[rows, :].astype(BF16), w_peer[...]
        )
        hidden = tok[rows, :].astype(F32) + (attn + out_bias[...])
        hidden_out[rows, :] = hidden
        xhat, _ = norm_stats(hidden)
        ln = (xhat * gain + shift).astype(BF16)
        ln_out[rows, :] = ln
        field[rows, :] = dot(ln, q_w[...]) + q_b[...]
        return carry

    lax.fori_loop(0, count // step, project, 0)
    for pair in range(pairs):
        columns = slice(pair * LANES, (pair + 1) * LANES)
        query_out[:, columns] = pltpu.roll(field[:, columns], count - (STRETCH - 1), 0).astype(BF16)

    def block(index, carry):
        rows = pl.ds(pl.multiple_of(index * STRETCH, STRETCH), STRETCH)
        near = pl.ds(pl.multiple_of(picks[index, 0] * span, span), span)
        far = pl.ds(pl.multiple_of(picks[index, 1] * span, span), span)
        lse = jnp.zeros((STRETCH, LANES), F32)
        for pair in range(pairs):
            columns = slice(pair * LANES, (pair + 1) * LANES)
            values = slice(local + pair * LANES, local + (pair + 1) * LANES)
            query = two_heads(query_out[rows, columns] * BF16(0.125))
            keys = jnp.concatenate([kv[near, columns], kv[far, columns]], axis=0)
            vals = jnp.concatenate([kv[near, values], kv[far, values]], axis=0)
            scores = dot_t(query, keys)
            top = jnp.max(scores, axis=-1, keepdims=True)
            expo = jnp.exp(scores - top)
            total = jnp.sum(expo, axis=-1, keepdims=True)
            probs = (expo * (1.0 / total)).astype(BF16)
            field[rows, columns] = join_heads(dot(probs, vals))
            lse = put_columns(lse, top + jnp.log(total), 2 * pair)
        lse_out[rows, :] = lse
        return carry

    lax.fori_loop(0, picks.shape[0], block, 0)
    valid = valid_rows(count, info, slots)
    for pair in range(pairs):
        columns = slice(pair * LANES, (pair + 1) * LANES)
        kept = jnp.where(valid, field[:, columns], 0.0)
        mix_out[:, columns] = pltpu.roll(kept, STRETCH - 1, 0).astype(BF16).astype(F32)


def gelu_parts(field):
    upper = 0.5 * (1.0 + lax.erf(field * (1.0 / math.sqrt(2.0))))
    density = jnp.exp(field * field * -0.5) * (1.0 / math.sqrt(2.0 * math.pi))
    return field * upper, upper + field * density


def feed_forward(
    info, hidden_one, mix_own, mix_peer, w_own, w_near, w_far, out_bias, gains, shifts, in_w, in_b, out_w, end_bias, grad,
    hidden_out, ln_out, act_out, pre_out, keep_out, send_out, part_out, bias_out, w_peer,
):
    @pl.when(pl.program_id(0) == 0)
    def _():
        join_peer(w_peer, w_near, w_far, info[2])
        bias_out[...] = jnp.zeros_like(bias_out)

    half = keep_out.shape[1]
    own = pl.ds(pl.multiple_of(info[1] * half, LANES), half)
    peer = pl.ds(pl.multiple_of((1 - info[1]) * half, LANES), half)
    cross = dot(mix_own[...].astype(BF16), w_own[...]) + dot(mix_peer[...].astype(BF16), w_peer[...])
    hidden = hidden_one[...] + (cross + out_bias[...])
    hidden_out[...] = hidden
    xhat, _ = norm_stats(hidden)
    ln = (xhat * gains[2:3, :] + shifts[2:3, :]).astype(BF16)
    ln_out[...] = ln
    act, slope = gelu_parts(dot(ln, in_w[...]) + in_b[...])
    act = act.astype(BF16)
    act_out[...] = act
    grad_pre = (dot_t(grad[...], out_w[...]) * slope).astype(BF16)
    pre_out[...] = grad_pre
    bias_out[...] += jnp.sum(grad_pre.astype(F32), axis=0, keepdims=True)
    part_out[...] = dot_t(grad_pre, in_w[...])
    keep_out[...] = dot(act, out_w[:, own]) + (hidden_out[:, own] + end_bias[:, own])
    send_out[...] = dot(act, out_w[:, peer])


def cross_backward(
    slots, span, order, info, picks, part_own, part_peer, hidden, out_grad, gains, out_w, query, kv, lse,
    mix, ln, flat_store,
    grad_out, query_out, query_low, store_out, sums_out, q_bias_out, v_bias_out, keep_out, send_one, send_two,
    rows_grad, field, store, low_out, turned, ordered,
):
    count = hidden.shape[0]
    local = query.shape[1]
    pairs = local // LANES
    step = 256
    gain = gains[2:3, :]
    sums_out[...] = jnp.zeros_like(sums_out)
    store[...] = jnp.zeros_like(store)

    def project(index, carry):
        rows = pl.ds(pl.multiple_of(index * step, step), step)
        gradient = part_own[rows, :] + part_peer[rows, :]
        xhat, scale = norm_stats(hidden[rows, :])
        sums_out[0:1, :] += jnp.sum(gradient * xhat, axis=0, keepdims=True)
        sums_out[1:2, :] += jnp.sum(gradient, axis=0, keepdims=True)
        cotangent = out_grad[rows, :].astype(F32)
        sums_out[3:4, :] += jnp.sum(cotangent, axis=0, keepdims=True)
        two = cotangent + norm_back(xhat, scale, gain, gradient)
        grad_out[rows, :] = two
        low = two.astype(BF16)
        low_out[rows, :] = low
        sums_out[2:3, :] += jnp.sum(low.astype(F32), axis=0, keepdims=True)
        field[rows, :] = dot_t(low, out_w[...])
        return carry

    lax.fori_loop(0, count // step, project, 0)
    valid = valid_rows(count, info, slots)
    for pair in range(pairs):
        columns = slice(pair * LANES, (pair + 1) * LANES)
        moved = pltpu.roll(field[:, columns].astype(BF16).astype(F32), count - (STRETCH - 1), 0)
        rows_grad[:, columns] = jnp.where(valid, moved, 0.0).astype(BF16)

    def block(index, carry):
        rows = pl.ds(pl.multiple_of(index * STRETCH, STRETCH), STRETCH)
        near = pl.ds(pl.multiple_of(picks[index, 0] * span, span), span)
        far = pl.ds(pl.multiple_of(picks[index, 1] * span, span), span)
        logs = lse[rows, :]
        for pair in range(pairs):
            columns = slice(pair * LANES, (pair + 1) * LANES)
            values = slice(local + pair * LANES, local + (pair + 1) * LANES)
            query_two = two_heads(query[rows, columns] * BF16(0.125))
            grad_two = two_heads(rows_grad[rows, columns])
            keys = jnp.concatenate([kv[near, columns], kv[far, columns]], axis=0)
            vals = jnp.concatenate([kv[near, values], kv[far, values]], axis=0)
            probs = jnp.exp(dot_t(query_two, keys) - two_columns(logs, 2 * pair))
            grad_probs = dot_t(grad_two, vals)
            delta = jnp.sum(probs * grad_probs, axis=-1, keepdims=True)
            grad_scores = (probs * (grad_probs - delta)).astype(BF16)
            field[rows, columns] = join_heads(dot(grad_scores, keys)) * 0.125
            grad_keys = tdot(grad_scores, query_two)
            grad_vals = tdot(probs.astype(BF16), grad_two)
            store[near, columns] += grad_keys[:span]
            store[far, columns] += grad_keys[span:]
            store[near, values] += grad_vals[:span]
            store[far, values] += grad_vals[span:]
        return carry

    lax.fori_loop(0, picks.shape[0], block, 0)
    for pair in range(pairs):
        columns = slice(pair * LANES, (pair + 1) * LANES)
        low = pltpu.roll(field[:, columns], STRETCH - 1, 0).astype(BF16)
        query_low[:, columns] = low
        query_out[:, columns] = low.astype(F32)
        q_bias_out[:, columns] = jnp.sum(low.astype(F32), axis=0, keepdims=True)

    v_bias_out[...] = jnp.zeros_like(v_bias_out)

    def flush(index, carry):
        rows = pl.ds(pl.multiple_of(index * span, span), span)
        low = store[rows, :].astype(BF16)
        store_out[rows, :] = low
        v_bias_out[...] += jnp.sum(low[:, local:].astype(F32), axis=0, keepdims=True)
        return carry

    lax.fori_loop(0, store.shape[0] // span, flush, 0)
    terms = ((low_out, mix), (ln, query_low), (flat_store, store_out))
    fill_grads(order, info[3 + slots], terms, keep_out, (send_one, send_two), turned, ordered)


def self_backward(
    slots, order, info, query_own, query_peer, q_w, q_near, q_far, hidden, grad_two, gains, out_w, qkv, lse, mask, cosine, sine, w,
    tok, cross_sums, q_bias, v_bias, in_bias, out_send, mix, ln,
    keep_out, send_out, grads_keep, grads_one, grads_two,
    q_peer, one, mix_grad, key_grad, value_grad, part, low_out, qkv_out, turned, ordered, sums_out,
):
    count = tok.shape[0]
    local = out_w.shape[0]
    pairs = local // LANES
    step = 256
    gain_one, gain_two = gains[0:1, :], gains[1:2, :]
    join_peer(q_peer, q_near, q_far, info[2])
    sums_out[...] = jnp.zeros_like(sums_out)
    half = keep_out.shape[1]
    own = pl.ds(pl.multiple_of(info[1] * half, LANES), half)
    peer = pl.ds(pl.multiple_of((1 - info[1]) * half, LANES), half)

    def project(index, carry):
        rows = pl.ds(pl.multiple_of(index * step, step), step)
        gradient = dot_t(query_own[rows, :], q_w[...]) + dot(
            query_peer[rows, :].astype(BF16), q_peer[...]
        )
        xhat, scale = norm_stats(hidden[rows, :])
        sums_out[2:3, :] += jnp.sum(gradient * xhat, axis=0, keepdims=True)
        sums_out[3:4, :] += jnp.sum(gradient, axis=0, keepdims=True)
        grad_one = grad_two[rows, :] + norm_back(xhat, scale, gain_two, gradient)
        one[rows, :] = grad_one
        low = grad_one.astype(BF16)
        low_out[rows, :] = low
        sums_out[4:5, :] += jnp.sum(low.astype(F32), axis=0, keepdims=True)
        mixed = dot_t(low, out_w[...])
        for pair in range(pairs):
            mix_grad[pair, rows, :] = mixed[:, pair * LANES : (pair + 1) * LANES].astype(BF16)
        return carry

    lax.fori_loop(0, count // step, project, 0)

    def attend(pair, carry):
        key_grad[...] = jnp.zeros_like(key_grad)
        value_grad[...] = jnp.zeros_like(value_grad)
        for start in range(0, count, TILE):
            rows = slice(start, start + TILE)
            until = slice(0, start + TILE)
            query = two_heads(qkv[pair, rows, :] * BF16(0.125))
            keys = qkv[pairs + pair, until, :]
            vals = qkv[2 * pairs + pair, until, :]
            grad_mix = two_heads(mix_grad[pair, rows, :])
            allowed = mask[rows, until]
            scores = dot_t(query, keys) + jnp.concatenate([allowed, allowed], axis=0)
            probs = jnp.exp(scores - two_columns(lse[rows, :], 2 * pair))
            grad_probs = dot_t(grad_mix, vals)
            delta = jnp.sum(probs * grad_probs, axis=-1, keepdims=True)
            grad_scores = (probs * (grad_probs - delta)).astype(BF16)
            grad_query = join_heads(dot(grad_scores, keys)) * 0.125
            back = turn(grad_query, cosine[rows, :], sine[rows, :], -1.0)
            qkv_out[pair, rows, :] = back.astype(BF16)
            key_grad[until, :] += tdot(grad_scores, query)
            value_grad[until, :] += tdot(probs.astype(BF16), grad_mix)
        for start in range(0, count, TILE):
            rows = slice(start, start + TILE)
            back = turn(key_grad[rows, :], cosine[rows, :], sine[rows, :], -1.0)
            qkv_out[pairs + pair, rows, :] = back.astype(BF16)
            qkv_out[2 * pairs + pair, rows, :] = value_grad[rows, :].astype(BF16)
        return carry

    lax.fori_loop(0, pairs, attend, 0)

    sums_out[5:9, :] = cross_sums[0:4, :]

    def place(piece, columns):
        start = (piece % 2) * local
        sums_out[9 + piece // 2 : 10 + piece // 2, start : start + local] = columns

    for part_at in range(3):
        place(
            part_at,
            jnp.concatenate(
                [
                    jnp.sum(qkv_out[part_at * pairs + pair].astype(F32), axis=0, keepdims=True)
                    for pair in range(pairs)
                ],
                axis=1,
            ),
        )
    place(3, q_bias[...])
    place(4, v_bias[...])
    for piece in range(in_bias.shape[1] // local):
        place(5 + piece, in_bias[:, piece * local : (piece + 1) * local])

    def finish(index, carry):
        rows = pl.ds(pl.multiple_of(index * step, step), step)
        gradient = jnp.zeros((step, tok.shape[1]), F32)
        for part_at in range(3):
            joined = jnp.concatenate(
                [qkv_out[part_at * pairs + pair, rows, :] for pair in range(pairs)], axis=1
            )
            gradient = gradient + dot_t(joined, w[part_at])
        xhat, scale = norm_stats(tok[rows, :].astype(F32))
        sums_out[0:1, :] += jnp.sum(gradient * xhat, axis=0, keepdims=True)
        sums_out[1:2, :] += jnp.sum(gradient, axis=0, keepdims=True)
        part[...] = norm_back(xhat, scale, gain_one, gradient)
        keep_out[rows, :] = part[:, own] + one[rows, own]
        send_out[rows, :half] = part[:, peer]
        send_out[rows, half:] = out_send[rows, :]
        return carry

    lax.fori_loop(0, count // step, finish, 0)
    terms = ((low_out, mix), (ln, qkv_out.at[:pairs]), (ln, qkv_out.at[pairs:]))
    fill_grads(order, info[3 + slots], terms, grads_keep, (grads_one, grads_two), turned, ordered)
    rows, wide = ordered.shape[0] // 2, sums_out.shape[1]
    grads_keep[rows:, :wide] = sums_out[0:RIDE, :]
    grads_keep[rows:, wide:] = sums_out[RIDE:, :]
    grads_one[rows:, :] = sums_out[0:RIDE, :]
    grads_two[rows:, :] = sums_out[RIDE:, :]


def slice_at(place, order):
    last = len(order) - 1
    return sum(bit * ((place >> (last - at)) & 1) for at, bit in enumerate(order))


def fill_grads(orders, me, terms, keep_out, send_outs, turned, ordered):
    width = turned.shape[0]
    half = width // 2
    share = send_outs[0].shape[1]
    column = 0
    for at_term, (left, right) in enumerate(terms):
        count = left.shape[0]
        if orders is None:
            ordered[:, :count] = left[...].T
        else:
            order = orders[at_term % len(orders)]
            parts = 1 << len(order)
            slab = width // parts
            if at_term == 0 or left is not terms[at_term - 1][0]:
                turned[:, :count] = left[...].T

            def move(place, carry, count=count, order=order):
                source = pl.multiple_of((me ^ slice_at(place, order)) * slab, 16)
                target = pl.multiple_of(place * slab, 16)
                ordered[pl.ds(target, slab), :count] = turned[pl.ds(source, slab), :count]
                return carry

            lax.fori_loop(0, parts, move, 0)
        pieces = right.shape[0] if len(right.shape) == 3 else right.shape[1] // LANES
        group = 3
        wide = group * LANES
        for index in range(pieces // group):
            if len(right.shape) == 3:
                field = jnp.concatenate([right[index * group + at] for at in range(group)], axis=1)
            else:
                field = right[:, index * wide : (index + 1) * wide]
            field = field.astype(BF16)
            keep_out[:half, column : column + wide] = dot(ordered[:half, :count], field)
            at = column % share
            send_outs[column // share][:half, at : at + wide] = dot(ordered[half:, :count], field)
            column += wide


def weight_grads(order, me_at, info, *refs):
    products = (len(refs) - 7) // 2
    lefts, rights = refs[:products], refs[products : 2 * products]
    keep_out, *send_outs = refs[2 * products : -2]
    fill_grads(order, info[me_at], tuple(zip(lefts, rights)), keep_out, send_outs, *refs[-2:])


def add_halves(pieces, joined, split, *refs):
    kept, came = refs[:2], refs[2 : 2 + 2 * pieces]
    outs = refs[2 + 2 * pieces + (2 if joined else 0) :]
    share = came[0].shape[1]
    for side in range(2):
        for piece in range(pieces):
            start = piece * share
            value = kept[side][:, start : start + share] + came[2 * piece + side][...]
            if start < split:
                outs[side][:, start : start + share] = value
            else:
                outs[2 + side][:, start - split : start - split + share] = value
        if joined:
            outs[side][:, pieces * share :] = refs[2 + 2 * pieces + side][...]


def whole(count):
    return [pl.BlockSpec(memory_space=pltpu.VMEM)] * count


def scalars(count):
    return [pl.BlockSpec(memory_space=pltpu.SMEM)] * count


def shape(dims, kind=F32):
    return jax.ShapeDtypeStruct(dims, kind)


def after(value, *others):
    return lax.optimization_barrier((value, *others))[0]


def work(flops):
    return pl.CostEstimate(flops=flops, bytes_accessed=1, transcendentals=0)


def call(body, name, small, big, outs, scratch=(), flops=0):
    return pl.pallas_call(
        body,
        name=name,
        out_shape=outs,
        in_specs=scalars(len(small)) + whole(len(big)),
        out_specs=whole(len(outs)),
        scratch_shapes=scratch,
        cost_estimate=work(flops),
    )(*small, *big)


def per_device(
    tokens,
    neighbours,
    out_grad,
    group_sizes,
    seq_lengths,
    stretch_neighbours,
    norm_gain,
    norm_bias,
    self_qkv_w,
    self_qkv_b,
    self_out_w,
    self_out_b,
    cross_q_w,
    cross_q_b,
    cross_kv_w,
    cross_v_b,
    cross_out_w,
    cross_out_b,
    mlp_in_w,
    mlp_in_b,
    mlp_out_w,
    mlp_out_b,
):
    count, width = tokens.shape
    local = self_qkv_w.shape[2]
    hidden = mlp_in_w.shape[1]
    pairs = local // LANES
    stored, span = neighbours.shape[:2]
    slots = seq_lengths.shape[1]
    dp_size = lax.axis_size("dp")
    slab = width // dp_size
    tp_at = lax.axis_index("tp")
    dp_at = lax.axis_index("dp")
    core = dp_at % 2

    def swap(value):
        return lax.ppermute(value, "tp", [(0, 1), (1, 0)])

    def across(value, bit):
        return lax.ppermute(value, "dp", [(at, at ^ bit) for at in range(dp_size)])

    def mine(weight):
        half = weight.shape[0] // 2
        return lax.dynamic_slice_in_dim(weight, core * half, half, 0).astype(F32)

    def mine_turned(weight):
        half = weight.shape[1] // 2
        return lax.dynamic_slice_in_dim(weight, core * half, half, 1).T.astype(F32)

    def row(value):
        return value.reshape(1, -1)

    padded = count // group_sizes[0]
    info = jnp.concatenate(
        [
            jnp.stack([padded, tp_at.astype(jnp.int32), core.astype(jnp.int32)]),
            seq_lengths[0],
            dp_at.astype(jnp.int32)[None],
        ]
    )
    position = (jnp.arange(count, dtype=jnp.int32) % padded).astype(F32)
    halfway = HEAD_DIM // 2
    frequency = jnp.exp(-math.log(10000.0) * jnp.arange(halfway, dtype=F32) / halfway)
    angles = position[:, None] * jnp.tile(frequency, LANES // halfway)[None, :]
    cosine = jnp.cos(angles)
    sine = jnp.sin(angles)

    bits = [1 << at for at in range(dp_size.bit_length() - 1)]
    far_first = bits[:1] + bits[2:] + bits[1:2]
    order = [bits] if slab % 16 == 0 else None
    mixed_order = [bits, bits, far_first] if slab % 16 == 0 else None

    def add_sent(name, kept, came, joined=(), split=None):
        rows, total = kept.shape[0] // 2, kept.shape[1]
        split = split or total
        steps = 4
        block = rows // steps

        def sides(value):
            wide = value.shape[1]
            return [
                pl.BlockSpec((block, wide), lambda i: (i, 0)),
                pl.BlockSpec((block, wide), lambda i: (i + steps, 0)),
            ]

        straight = lambda wide: pl.BlockSpec((block, wide), lambda i: (i, 0))
        first = split + sum(value.shape[1] for value in joined[:1])
        wides = [first, first] + ([total - split] * 2 if split < total else [])
        return pl.pallas_call(
            partial(add_halves, len(came), bool(joined), split),
            name=name,
            grid=(steps,),
            in_specs=[spec for value in (kept, *came) for spec in sides(value)]
            + [straight(value.shape[1]) for value in joined],
            out_specs=[straight(wide) for wide in wides],
            out_shape=[shape((rows, wide)) for wide in wides],
            cost_estimate=work(0),
        )(*[value for value in (kept, *came) for _ in range(2)], *joined)

    def sorted_halves(kept, *sent, orders=(bits,)):
        if slab % 16 == 0:
            return kept, sent
        half = width // 2
        value = jnp.concatenate([kept[:half], jnp.concatenate([piece[:half] for piece in sent], axis=1)], axis=0)
        made = []
        for part, wanted in zip(jnp.split(value, len(orders), axis=1), orders):
            places = jnp.array([slice_at(place, wanted) for place in range(dp_size)], jnp.int32) ^ dp_at
            made.append(jnp.take(part.reshape(dp_size, slab, -1), places, axis=0).reshape(part.shape))
        value = jnp.concatenate(made, axis=1)
        fresh = jnp.split(value[half:], len(sent), axis=1)
        sent = [jnp.concatenate([new, old[half:]], axis=0) for new, old in zip(fresh, sent)]
        return jnp.concatenate([value[:half], kept[half:]], axis=0), sent

    def ride_on(kept, sent, bit):
        came = across(sent, bit)
        half = kept.shape[0] // 2
        far = jnp.concatenate([kept[half:], sent[-RIDE:]], axis=0)
        return kept[:half] + came[:half], far + came[half:]

    def core_halve(halves, gate=None):
        kept, sent = halves
        came = jnp.concatenate([across(piece, 1) for piece in sent], axis=1)
        return merge(kept if gate is None else after(kept, *gate), came)

    def grads_of(total, shares, more=0):
        rows = width // 2 + more
        return (shape((rows, total)),) + (shape((rows, total // shares)),) * shares

    def turning(most):
        return [pltpu.VMEM((width, most), BF16), pltpu.VMEM((width, most), BF16)]

    def merge(kept, arrived):
        half = kept.shape[0] // 2
        return kept[:half] + arrived[:half], kept[half:] + arrived[half:]

    def halve(kept, sent, bit):
        return merge(kept, across(sent, bit))

    so_near = swap(mine(self_out_w))
    qkv_w = jnp.swapaxes(self_qkv_w, 0, 1)
    ln_one, qkv, self_mix, self_lse, mask = call(
        partial(self_forward, slots),
        "self_forward",
        (info,),
        (tokens, qkv_w, self_qkv_b, norm_gain, norm_bias, cosine, sine),
        (
            shape((count, width), BF16),
            shape((3 * pairs, count, LANES), BF16),
            shape((count, local)),
            shape((count, LANES)),
            shape((count, count)),
        ),
        flops=11_000_000_000,
    )
    self_mix_peer = swap(self_mix)
    so_far = across(so_near, 1)

    kv_w = jnp.swapaxes(cross_kv_w, 0, 1).reshape(2, width, local)
    flat_store = neighbours.reshape(stored * span, width)
    kv_bias = jnp.concatenate([jnp.zeros_like(cross_v_b), cross_v_b])
    joined_kv = jnp.concatenate([kv_w[0], kv_w[1]], axis=1)
    store_kv = (dot(flat_store, joined_kv) + kv_bias).astype(BF16)

    co_near = swap(after(mine(cross_out_w), self_mix_peer))
    hidden_one, ln_two, cross_query, cross_mix, cross_lse = call(
        partial(cross_forward, slots, span),
        "cross_forward",
        (info, stretch_neighbours),
        (
            tokens,
            self_mix,
            self_mix_peer,
            self_out_w,
            so_near,
            so_far,
            row(self_out_b),
            norm_gain,
            norm_bias,
            cross_q_w,
            row(cross_q_b),
            store_kv,
        ),
        (
            shape((count, width)),
            shape((count, width), BF16),
            shape((count, local), BF16),
            shape((count, local)),
            shape((count, LANES)),
        ),
        [pltpu.VMEM((local, width), BF16), pltpu.VMEM((count, local), F32)],
        flops=14_000_000_000,
    )
    cross_mix_peer = swap(cross_mix)
    co_far = across(co_near, 1)
    cq_near = swap(after(mine_turned(cross_q_w), cross_mix_peer))

    step = 256
    rows = lambda wide: pl.BlockSpec((step, wide), lambda i: (i, 0))
    kept = pl.BlockSpec(memory_space=pltpu.VMEM)
    own_width = width // 2
    hidden_two, ln_three, act, grad_pre, out_keep, out_send, part_three, mlp_in_b_grad = pl.pallas_call(
        feed_forward,
        name="feed_forward",
        grid=(count // step,),
        in_specs=[pl.BlockSpec(memory_space=pltpu.SMEM), rows(width), rows(local), rows(local)]
        + [kept] * 10
        + [rows(width)],
        out_specs=[
            rows(width),
            rows(width),
            rows(hidden),
            rows(hidden),
            rows(own_width),
            rows(own_width),
            rows(width),
            pl.BlockSpec((1, hidden), lambda i: (0, 0)),
        ],
        out_shape=[
            shape((count, width)),
            shape((count, width), BF16),
            shape((count, hidden), BF16),
            shape((count, hidden), BF16),
            shape((count, own_width)),
            shape((count, own_width)),
            shape((count, width)),
            shape((1, hidden)),
        ],
        scratch_shapes=[pltpu.VMEM((local, width), BF16)],
        cost_estimate=work(14_000_000_000),
    )(
        info,
        hidden_one,
        cross_mix,
        cross_mix_peer,
        cross_out_w,
        co_near,
        co_far,
        row(cross_out_b),
        norm_gain,
        norm_bias,
        mlp_in_w,
        row(mlp_in_b),
        mlp_out_w,
        row(mlp_out_b),
        out_grad,
    )
    part_three_peer = swap(part_three)
    cq_far = across(cq_near, 1)
    mlp = sorted_halves(
        *call(
            partial(weight_grads, order, 3 + slots),
            "mlp_grads",
            (info,),
            (after(out_grad, cq_near), ln_three, act, grad_pre),
            grads_of(2 * hidden, 4),
            turning(count),
            flops=0,
        )
    )
    came_mlp = [across(piece, 1) for piece in mlp[1]]
    first = add_sent("add_mlp", mlp[0], came_mlp)
    (
        grad_two,
        grad_query,
        grad_query_low,
        grad_store,
        cross_sums,
        cross_q_b_grad,
        cross_v_b_grad,
        *cross_halves,
    ) = call(
        partial(cross_backward, slots, span, order),
        "cross_backward",
        (info, stretch_neighbours),
        (
            part_three,
            part_three_peer,
            after(hidden_two, first[1]),
            out_grad,
            norm_gain,
            cross_out_w,
            cross_query,
            store_kv,
            cross_lse,
            cross_mix,
            ln_two,
            flat_store,
        ),
        (
            shape((count, width)),
            shape((count, local)),
            shape((count, local), BF16),
            shape((stored * span, 2 * local), BF16),
            shape((8, width)),
            shape((1, local)),
            shape((1, local)),
            *grads_of(4 * local, 2),
        ),
        [
            pltpu.VMEM((count, local), BF16),
            pltpu.VMEM((count, local), F32),
            pltpu.VMEM((stored * span, 2 * local), F32),
            pltpu.VMEM((count, width), BF16),
            *turning(max(count, stored * span)),
        ],
        flops=17_000_000_000,
    )
    grad_query_peer = swap(grad_query)
    first = halve(*first, bits[1])

    own_kv = lax.dynamic_slice_in_dim(joined_kv, tp_at * own_width, own_width, 0)
    peer_kv = lax.dynamic_slice_in_dim(joined_kv, (1 - tp_at) * own_width, own_width, 0)
    store_send = dot_t(grad_store, peer_kv)
    store_keep = dot_t(grad_store, own_kv)
    cross = sorted_halves(*cross_halves)
    came_cross = [across(piece, 1) for piece in cross[1]]
    third = add_sent("add_cross", cross[0], came_cross)
    store_back = swap(after(store_send, third[1]))

    tok_keep, both_send, *self_halves = call(
        partial(self_backward, slots, mixed_order),
        "self_backward",
        (info,),
        (
            grad_query_low,
            grad_query_peer,
            cross_q_w,
            cq_near,
            cq_far,
            hidden_one,
            after(grad_two, third[1], first[1]),
            norm_gain,
            self_out_w,
            qkv,
            self_lse,
            mask,
            cosine,
            sine,
            qkv_w,
            tokens,
            cross_sums,
            cross_q_b_grad,
            cross_v_b_grad,
            mlp_in_b_grad,
            out_send,
            self_mix,
            ln_one,
        ),
        (
            shape((count, own_width)),
            shape((count, width)),
            *grads_of(4 * local, 2, RIDE),
        ),
        [
            pltpu.VMEM((local, width), BF16),
            pltpu.VMEM((count, width), F32),
            pltpu.VMEM((pairs, count, LANES), BF16),
            pltpu.VMEM((count, LANES), F32),
            pltpu.VMEM((count, LANES), F32),
            pltpu.VMEM((256, width), F32),
            pltpu.VMEM((count, width), BF16),
            pltpu.VMEM((3 * pairs, count, LANES), BF16),
            *turning(count),
            pltpu.VMEM((2 * RIDE, width), F32),
        ],
        flops=40_000_000_000,
    )
    back = swap(both_send)
    neighbours_grad = (store_keep + store_back).astype(BF16)

    first = halve(after(first[0], self_halves[0]), first[1], bits[2])
    third_came = across(third[1], bits[1])
    third = merge(after(third[0], self_halves[0]), third_came)
    kept, sent = sorted_halves(*self_halves, orders=(bits, far_first))
    kept = after(kept, first[1], third[1])
    half, middle = width // 4, 2 * local

    def ride_core(kept, sent):
        came = across(sent, 1)
        return kept[:half] + came[:half], kept[half:] + came[half:]

    def ride_end(kept, sent, order):
        for bit in order[:-1]:
            kept, sent = ride_on(kept, sent, bit)
        came = across(sent, order[-1])
        return kept + came[:slab], sent[-RIDE:] + came[slab:]

    near_part = ride_core(kept[:, :middle], sent[0])
    far_part = ride_core(kept[:, middle:], sent[1])
    third = after(third[0], near_part[1], far_part[1]), third[1]
    first = after(first[0], near_part[1], far_part[1]), first[1]
    near_part = ride_on(*near_part, bits[1])
    far_part = ride_on(*far_part, far_first[1])
    done = near_part[1], far_part[1]
    near_part, low_sums = ride_end(*near_part, bits[2:])
    far_part, high_sums = ride_end(*far_part, far_first[2:])
    self_grads = jnp.concatenate([near_part, far_part], axis=1)
    sums = jnp.concatenate([low_sums, high_sums], axis=0)

    back = after(back, *done)
    tokens_grad = (tok_keep + back[:, :own_width]).astype(BF16)
    output = (out_keep + back[:, own_width:]).astype(BF16)

    def finish(parts, order):
        for bit in order[:-1]:
            parts = halve(*parts, bit)
        return after(parts[0], *done) + across(parts[1], order[-1])

    mlp_grads = finish(first, bits[3:])
    cross_grads = finish(third, bits[2:])
    mlp_out_w_grad, mlp_in_w_grad = mlp_grads[:, :hidden], mlp_grads[:, hidden:]

    shared = 0.5 * sums[2:9]
    shared = jnp.concatenate([sums[0:2], shared], axis=0)
    shared = shared + swap(shared)
    alone = sums[9:].reshape(-1)
    return (
        output,
        tokens_grad,
        neighbours_grad.reshape(stored, span, own_width),
        jnp.stack([shared[0], shared[2], shared[5]]),
        jnp.stack([shared[1], shared[3], shared[6]]),
        self_grads[:, local:].reshape(-1, 3, local),
        alone[: 3 * local].reshape(3, local),
        self_grads[:, :local].T,
        shared[4],
        cross_grads[:, local : 2 * local],
        alone[3 * local : 4 * local],
        cross_grads[:, 2 * local :].reshape(-1, 2, local),
        alone[4 * local : 5 * local],
        cross_grads[:, :local].T,
        shared[7],
        mlp_in_w_grad,
        alone[5 * local : 5 * local + hidden],
        mlp_out_w_grad.T,
        shared[8],
    )


def solution(mesh):
    placed = (
        P("dp", None),
        P("dp", None, None),
        P("dp", None),
        P("dp"),
        P("dp", None),
        P("dp", None),
        P(),
        P(),
        P(None, None, "tp"),
        P(None, "tp"),
        P("tp", None),
        P(),
        P(None, "tp"),
        P("tp"),
        P(None, None, "tp"),
        P("tp"),
        P("tp", None),
        P(),
        P(None, "tp"),
        P("tp"),
        P("tp", None),
        P(),
    )
    return jax.shard_map(
        per_device,
        mesh=mesh,
        in_specs=placed,
        out_specs=(
            P("dp", "tp"),
            P("dp", "tp"),
            P("dp", None, "tp"),
            P(),
            P(),
            P("dp", None, "tp"),
            P(None, "tp"),
            P("tp", "dp"),
            P(),
            P("dp", "tp"),
            P("tp"),
            P("dp", None, "tp"),
            P("tp"),
            P("tp", "dp"),
            P(),
            P("dp", "tp"),
            P("tp"),
            P("tp", "dp"),
            P(),
        ),
        check_vma=False,
    )
```

```python
from functools import partial
import math

import jax
import jax.numpy as jnp
from jax import lax
from jax.experimental import pallas as pl
from jax.experimental.pallas import tpu as pltpu
from jax.sharding import PartitionSpec as P

HEAD_DIM = 64
STRETCH = 64
LANES = 128
F32 = jnp.float32
BF16 = jnp.bfloat16
TILE = 128
RIDE = 8


def dot(left, right):
    return lax.dot_general(left, right, (((1,), (0,)), ((), ())), preferred_element_type=F32)


def dot_t(left, right):
    return lax.dot_general(left, right, (((1,), (1,)), ((), ())), preferred_element_type=F32)


def tdot(left, right):
    return lax.dot_general(left, right, (((0,), (0,)), ((), ())), preferred_element_type=F32)


def norm_stats(field):
    center = field - jnp.mean(field, axis=-1, keepdims=True)
    spread = jnp.mean(center * center, axis=-1, keepdims=True)
    scale = lax.rsqrt(spread + 1e-05)
    return center * scale, scale


def norm_back(xhat, scale, gain, gradient):
    scaled = gradient * gain
    first = jnp.mean(scaled, axis=-1, keepdims=True)
    second = jnp.mean(scaled * xhat, axis=-1, keepdims=True)
    return scale * (scaled - first - xhat * second)


def lane_ids(rows):
    return lax.broadcasted_iota(jnp.int32, (rows, LANES), 1)


def turn(field, cosine, sine, direction):
    lane = lane_ids(field.shape[0])
    ahead = pltpu.roll(field, LANES - HEAD_DIM // 2, 1)
    behind = pltpu.roll(field, HEAD_DIM // 2, 1)
    crossed = jnp.where((lane & (HEAD_DIM - 1)) < HEAD_DIM // 2, -ahead, behind)
    return field * cosine + crossed * (sine * direction)


def two_heads(field):
    low = lane_ids(field.shape[0]) < HEAD_DIM
    zero = jnp.zeros_like(field)
    return jnp.concatenate([jnp.where(low, field, zero), jnp.where(low, zero, field)], axis=0)


def join_heads(field):
    half = field.shape[0] // 2
    return jnp.where(lane_ids(half) < HEAD_DIM, field[:half], field[half:])


def two_columns(columns, first):
    lane = lane_ids(columns.shape[0])
    parts = [
        jnp.sum(jnp.where(lane == first + head, columns, 0.0), axis=-1, keepdims=True)
        for head in range(2)
    ]
    return jnp.concatenate(parts, axis=0)


def put_columns(columns, values, first):
    half = columns.shape[0]
    lane = lane_ids(half)
    columns = jnp.where(lane == first, values[:half], columns)
    return jnp.where(lane == first + 1, values[half:], columns)


def slot_length(ids, info, slots):
    length = jnp.zeros_like(ids)
    for slot in range(slots):
        length = jnp.where(ids >= slot * info[0], info[3 + slot], length)
    return length


def fill_mask(bias_ref, info, slots):
    count = bias_ref.shape[0]
    padded = info[0]
    for start in range(0, count, TILE):
        shape = (TILE, start + TILE)
        rows = lax.broadcasted_iota(jnp.int32, shape, 0) + start
        keys = lax.broadcasted_iota(jnp.int32, shape, 1)
        place = keys & (padded - 1)
        allowed = (
            (keys <= rows)
            & (keys >= rows - (rows & (padded - 1)))
            & (place < slot_length(keys, info, slots))
        )
        bias_ref[start : start + TILE, : start + TILE] = jnp.where(allowed, 0.0, -1e30)


def valid_rows(count, info, slots):
    rows = lax.broadcasted_iota(jnp.int32, (count, LANES), 0)
    shifted = (rows & (info[0] - 1)) + (STRETCH - 1)
    return (shifted < info[0]) & (shifted < slot_length(rows, info, slots))


def join_peer(peer_ref, near_ref, far_ref, core):
    half = peer_ref.shape[0] // 2
    peer_ref[pl.ds(pl.multiple_of(core * half, 64), half), :] = near_ref[...].astype(BF16)
    peer_ref[pl.ds(pl.multiple_of((1 - core) * half, 64), half), :] = far_ref[...].astype(BF16)


def self_forward(slots, info, tok, weight, bias, gains, shifts, cosine, sine, ln_out, qkv_out, mix_out, lse_out, mask_out):
    count = tok.shape[0]
    pairs = weight.shape[2] // LANES
    gain, shift = gains[0:1, :], shifts[0:1, :]
    fill_mask(mask_out, info, slots)
    step = 256

    def project(index, carry):
        rows = pl.ds(pl.multiple_of(index * step, step), step)
        xhat, _ = norm_stats(tok[rows, :].astype(F32))
        ln = (xhat * gain + shift).astype(BF16)
        ln_out[rows, :] = ln
        for part in range(3):
            made = dot(ln, weight[part]) + bias[part : part + 1, :]
            for pair in range(pairs):
                piece = made[:, pair * LANES : (pair + 1) * LANES]
                if part < 2:
                    piece = turn(piece, cosine[rows, :], sine[rows, :], 1.0)
                qkv_out[part * pairs + pair, rows, :] = piece.astype(BF16)
        return carry

    lax.fori_loop(0, count // step, project, 0)

    def attend(pair, carry):
        columns = pl.ds(pl.multiple_of(pair * LANES, LANES), LANES)
        for start in range(0, count, TILE):
            rows = slice(start, start + TILE)
            span = slice(0, start + TILE)
            query = two_heads(qkv_out[pair, rows, :] * BF16(0.125))
            scores = dot_t(query, qkv_out[pairs + pair, span, :])
            mask = mask_out[rows, span]
            scores = scores + jnp.concatenate([mask, mask], axis=0)
            top = jnp.max(scores, axis=-1, keepdims=True)
            expo = jnp.exp(scores - top)
            total = jnp.sum(expo, axis=-1, keepdims=True)
            probs = (expo * (1.0 / total)).astype(BF16)
            mixed = join_heads(dot(probs, qkv_out[2 * pairs + pair, span, :]))
            mix_out[rows, columns] = mixed.astype(BF16).astype(F32)
            lse_out[rows, :] = put_columns(lse_out[rows, :], top + jnp.log(total), 2 * pair)
        return carry

    lax.fori_loop(0, pairs, attend, 0)


def cross_forward(
    slots, span, info, picks, tok, mix_own, mix_peer, w_own, w_near, w_far, out_bias, gains, shifts, q_w, q_b, kv,
    hidden_out, ln_out, query_out, mix_out, lse_out, w_peer, field,
):
    count = tok.shape[0]
    local = q_w.shape[1]
    pairs = local // LANES
    gain, shift = gains[1:2, :], shifts[1:2, :]
    join_peer(w_peer, w_near, w_far, info[2])
    step = 256

    def project(index, carry):
        rows = pl.ds(pl.multiple_of(index * step, step), step)
        attn = dot(mix_own[rows, :].astype(BF16), w_own[...]) + dot(
            mix_peer[rows, :].astype(BF16), w_peer[...]
        )
        hidden = tok[rows, :].astype(F32) + (attn + out_bias[...])
        hidden_out[rows, :] = hidden
        xhat, _ = norm_stats(hidden)
        ln = (xhat * gain + shift).astype(BF16)
        ln_out[rows, :] = ln
        field[rows, :] = dot(ln, q_w[...]) + q_b[...]
        return carry

    lax.fori_loop(0, count // step, project, 0)
    for pair in range(pairs):
        columns = slice(pair * LANES, (pair + 1) * LANES)
        query_out[:, columns] = pltpu.roll(field[:, columns], count - (STRETCH - 1), 0).astype(BF16)

    def block(index, carry):
        rows = pl.ds(pl.multiple_of(index * STRETCH, STRETCH), STRETCH)
        near = pl.ds(pl.multiple_of(picks[index, 0] * span, span), span)
        far = pl.ds(pl.multiple_of(picks[index, 1] * span, span), span)
        lse = jnp.zeros((STRETCH, LANES), F32)
        for pair in range(pairs):
            columns = slice(pair * LANES, (pair + 1) * LANES)
            values = slice(local + pair * LANES, local + (pair + 1) * LANES)
            query = two_heads(query_out[rows, columns] * BF16(0.125))
            keys = jnp.concatenate([kv[near, columns], kv[far, columns]], axis=0)
            vals = jnp.concatenate([kv[near, values], kv[far, values]], axis=0)
            scores = dot_t(query, keys)
            top = jnp.max(scores, axis=-1, keepdims=True)
            expo = jnp.exp(scores - top)
            total = jnp.sum(expo, axis=-1, keepdims=True)
            probs = (expo * (1.0 / total)).astype(BF16)
            field[rows, columns] = join_heads(dot(probs, vals))
            lse = put_columns(lse, top + jnp.log(total), 2 * pair)
        lse_out[rows, :] = lse
        return carry

    lax.fori_loop(0, picks.shape[0], block, 0)
    valid = valid_rows(count, info, slots)
    for pair in range(pairs):
        columns = slice(pair * LANES, (pair + 1) * LANES)
        kept = jnp.where(valid, field[:, columns], 0.0)
        mix_out[:, columns] = pltpu.roll(kept, STRETCH - 1, 0).astype(BF16).astype(F32)


def gelu_parts(field):
    upper = 0.5 * (1.0 + lax.erf(field * (1.0 / math.sqrt(2.0))))
    density = jnp.exp(field * field * -0.5) * (1.0 / math.sqrt(2.0 * math.pi))
    return field * upper, upper + field * density


def feed_forward(
    info, hidden_one, mix_own, mix_peer, w_own, w_near, w_far, out_bias, gains, shifts, in_w, in_b, out_w, end_bias, grad,
    hidden_out, ln_out, act_out, pre_out, keep_out, send_out, part_out, bias_out, w_peer,
):
    @pl.when(pl.program_id(0) == 0)
    def _():
        join_peer(w_peer, w_near, w_far, info[2])
        bias_out[...] = jnp.zeros_like(bias_out)

    half = keep_out.shape[1]
    own = pl.ds(pl.multiple_of(info[1] * half, LANES), half)
    peer = pl.ds(pl.multiple_of((1 - info[1]) * half, LANES), half)
    cross = dot(mix_own[...].astype(BF16), w_own[...]) + dot(mix_peer[...].astype(BF16), w_peer[...])
    hidden = hidden_one[...] + (cross + out_bias[...])
    hidden_out[...] = hidden
    xhat, _ = norm_stats(hidden)
    ln = (xhat * gains[2:3, :] + shifts[2:3, :]).astype(BF16)
    ln_out[...] = ln
    act, slope = gelu_parts(dot(ln, in_w[...]) + in_b[...])
    act = act.astype(BF16)
    act_out[...] = act
    grad_pre = (dot_t(grad[...], out_w[...]) * slope).astype(BF16)
    pre_out[...] = grad_pre
    bias_out[...] += jnp.sum(grad_pre.astype(F32), axis=0, keepdims=True)
    part_out[...] = dot_t(grad_pre, in_w[...])
    keep_out[...] = dot(act, out_w[:, own]) + (hidden_out[:, own] + end_bias[:, own])
    send_out[...] = dot(act, out_w[:, peer])


def cross_backward(
    slots, span, order, info, picks, part_own, part_peer, hidden, out_grad, gains, out_w, query, kv, lse,
    mix, ln, flat_store,
    grad_out, query_out, query_low, store_out, sums_out, q_bias_out, v_bias_out, keep_out, send_one, send_two,
    rows_grad, field, store, low_out, turned, ordered,
):
    count = hidden.shape[0]
    local = query.shape[1]
    pairs = local // LANES
    step = 256
    gain = gains[2:3, :]
    sums_out[...] = jnp.zeros_like(sums_out)
    store[...] = jnp.zeros_like(store)

    def project(index, carry):
        rows = pl.ds(pl.multiple_of(index * step, step), step)
        gradient = part_own[rows, :] + part_peer[rows, :]
        xhat, scale = norm_stats(hidden[rows, :])
        sums_out[0:1, :] += jnp.sum(gradient * xhat, axis=0, keepdims=True)
        sums_out[1:2, :] += jnp.sum(gradient, axis=0, keepdims=True)
        cotangent = out_grad[rows, :].astype(F32)
        sums_out[3:4, :] += jnp.sum(cotangent, axis=0, keepdims=True)
        two = cotangent + norm_back(xhat, scale, gain, gradient)
        grad_out[rows, :] = two
        low = two.astype(BF16)
        low_out[rows, :] = low
        sums_out[2:3, :] += jnp.sum(low.astype(F32), axis=0, keepdims=True)
        field[rows, :] = dot_t(low, out_w[...])
        return carry

    lax.fori_loop(0, count // step, project, 0)
    valid = valid_rows(count, info, slots)
    for pair in range(pairs):
        columns = slice(pair * LANES, (pair + 1) * LANES)
        moved = pltpu.roll(field[:, columns].astype(BF16).astype(F32), count - (STRETCH - 1), 0)
        rows_grad[:, columns] = jnp.where(valid, moved, 0.0).astype(BF16)

    def block(index, carry):
        rows = pl.ds(pl.multiple_of(index * STRETCH, STRETCH), STRETCH)
        near = pl.ds(pl.multiple_of(picks[index, 0] * span, span), span)
        far = pl.ds(pl.multiple_of(picks[index, 1] * span, span), span)
        logs = lse[rows, :]
        for pair in range(pairs):
            columns = slice(pair * LANES, (pair + 1) * LANES)
            values = slice(local + pair * LANES, local + (pair + 1) * LANES)
            query_two = two_heads(query[rows, columns] * BF16(0.125))
            grad_two = two_heads(rows_grad[rows, columns])
            keys = jnp.concatenate([kv[near, columns], kv[far, columns]], axis=0)
            vals = jnp.concatenate([kv[near, values], kv[far, values]], axis=0)
            probs = jnp.exp(dot_t(query_two, keys) - two_columns(logs, 2 * pair))
            grad_probs = dot_t(grad_two, vals)
            delta = jnp.sum(probs * grad_probs, axis=-1, keepdims=True)
            grad_scores = (probs * (grad_probs - delta)).astype(BF16)
            field[rows, columns] = join_heads(dot(grad_scores, keys)) * 0.125
            grad_keys = tdot(grad_scores, query_two)
            grad_vals = tdot(probs.astype(BF16), grad_two)
            store[near, columns] += grad_keys[:span]
            store[far, columns] += grad_keys[span:]
            store[near, values] += grad_vals[:span]
            store[far, values] += grad_vals[span:]
        return carry

    lax.fori_loop(0, picks.shape[0], block, 0)
    for pair in range(pairs):
        columns = slice(pair * LANES, (pair + 1) * LANES)
        low = pltpu.roll(field[:, columns], STRETCH - 1, 0).astype(BF16)
        query_low[:, columns] = low
        query_out[:, columns] = low.astype(F32)
        q_bias_out[:, columns] = jnp.sum(low.astype(F32), axis=0, keepdims=True)

    v_bias_out[...] = jnp.zeros_like(v_bias_out)

    def flush(index, carry):
        rows = pl.ds(pl.multiple_of(index * span, span), span)
        low = store[rows, :].astype(BF16)
        store_out[rows, :] = low
        v_bias_out[...] += jnp.sum(low[:, local:].astype(F32), axis=0, keepdims=True)
        return carry

    lax.fori_loop(0, store.shape[0] // span, flush, 0)
    terms = ((low_out, mix), (ln, query_low), (flat_store, store_out))
    fill_grads(order, info[3 + slots], terms, keep_out, (send_one, send_two), turned, ordered)


def self_backward(
    slots, order, info, query_own, query_peer, q_w, q_near, q_far, hidden, grad_two, gains, out_w, qkv, lse, mask, cosine, sine, w,
    tok, cross_sums, q_bias, v_bias, in_bias, out_send, mix, ln,
    keep_out, send_out, grads_keep, grads_one, grads_two,
    q_peer, one, mix_grad, key_grad, value_grad, part, low_out, qkv_out, turned, ordered, sums_out,
):
    count = tok.shape[0]
    local = out_w.shape[0]
    pairs = local // LANES
    step = 256
    gain_one, gain_two = gains[0:1, :], gains[1:2, :]
    join_peer(q_peer, q_near, q_far, info[2])
    sums_out[...] = jnp.zeros_like(sums_out)
    half = keep_out.shape[1]
    own = pl.ds(pl.multiple_of(info[1] * half, LANES), half)
    peer = pl.ds(pl.multiple_of((1 - info[1]) * half, LANES), half)

    def project(index, carry):
        rows = pl.ds(pl.multiple_of(index * step, step), step)
        gradient = dot_t(query_own[rows, :], q_w[...]) + dot(
            query_peer[rows, :].astype(BF16), q_peer[...]
        )
        xhat, scale = norm_stats(hidden[rows, :])
        sums_out[2:3, :] += jnp.sum(gradient * xhat, axis=0, keepdims=True)
        sums_out[3:4, :] += jnp.sum(gradient, axis=0, keepdims=True)
        grad_one = grad_two[rows, :] + norm_back(xhat, scale, gain_two, gradient)
        one[rows, :] = grad_one
        low = grad_one.astype(BF16)
        low_out[rows, :] = low
        sums_out[4:5, :] += jnp.sum(low.astype(F32), axis=0, keepdims=True)
        mixed = dot_t(low, out_w[...])
        for pair in range(pairs):
            mix_grad[pair, rows, :] = mixed[:, pair * LANES : (pair + 1) * LANES].astype(BF16)
        return carry

    lax.fori_loop(0, count // step, project, 0)

    def attend(pair, carry):
        key_grad[...] = jnp.zeros_like(key_grad)
        value_grad[...] = jnp.zeros_like(value_grad)
        for start in range(0, count, TILE):
            rows = slice(start, start + TILE)
            until = slice(0, start + TILE)
            query = two_heads(qkv[pair, rows, :] * BF16(0.125))
            keys = qkv[pairs + pair, until, :]
            vals = qkv[2 * pairs + pair, until, :]
            grad_mix = two_heads(mix_grad[pair, rows, :])
            allowed = mask[rows, until]
            scores = dot_t(query, keys) + jnp.concatenate([allowed, allowed], axis=0)
            probs = jnp.exp(scores - two_columns(lse[rows, :], 2 * pair))
            grad_probs = dot_t(grad_mix, vals)
            delta = jnp.sum(probs * grad_probs, axis=-1, keepdims=True)
            grad_scores = (probs * (grad_probs - delta)).astype(BF16)
            grad_query = join_heads(dot(grad_scores, keys)) * 0.125
            back = turn(grad_query, cosine[rows, :], sine[rows, :], -1.0)
            qkv_out[pair, rows, :] = back.astype(BF16)
            key_grad[until, :] += tdot(grad_scores, query)
            value_grad[until, :] += tdot(probs.astype(BF16), grad_mix)
        for start in range(0, count, TILE):
            rows = slice(start, start + TILE)
            back = turn(key_grad[rows, :], cosine[rows, :], sine[rows, :], -1.0)
            qkv_out[pairs + pair, rows, :] = back.astype(BF16)
            qkv_out[2 * pairs + pair, rows, :] = value_grad[rows, :].astype(BF16)
        return carry

    lax.fori_loop(0, pairs, attend, 0)

    sums_out[5:9, :] = cross_sums[0:4, :]

    def place(piece, columns):
        start = (piece % 2) * local
        sums_out[9 + piece // 2 : 10 + piece // 2, start : start + local] = columns

    for part_at in range(3):
        place(
            part_at,
            jnp.concatenate(
                [
                    jnp.sum(qkv_out[part_at * pairs + pair].astype(F32), axis=0, keepdims=True)
                    for pair in range(pairs)
                ],
                axis=1,
            ),
        )
    place(3, q_bias[...])
    place(4, v_bias[...])
    for piece in range(in_bias.shape[1] // local):
        place(5 + piece, in_bias[:, piece * local : (piece + 1) * local])

    def finish(index, carry):
        rows = pl.ds(pl.multiple_of(index * step, step), step)
        gradient = jnp.zeros((step, tok.shape[1]), F32)
        for part_at in range(3):
            joined = jnp.concatenate(
                [qkv_out[part_at * pairs + pair, rows, :] for pair in range(pairs)], axis=1
            )
            gradient = gradient + dot_t(joined, w[part_at])
        xhat, scale = norm_stats(tok[rows, :].astype(F32))
        sums_out[0:1, :] += jnp.sum(gradient * xhat, axis=0, keepdims=True)
        sums_out[1:2, :] += jnp.sum(gradient, axis=0, keepdims=True)
        part[...] = norm_back(xhat, scale, gain_one, gradient)
        keep_out[rows, :] = part[:, own] + one[rows, own]
        send_out[rows, :half] = part[:, peer]
        send_out[rows, half:] = out_send[rows, :]
        return carry

    lax.fori_loop(0, count // step, finish, 0)
    terms = ((low_out, mix), (ln, qkv_out.at[:pairs]), (ln, qkv_out.at[pairs:]))
    fill_grads(order, info[3 + slots], terms, grads_keep, (grads_one, grads_two), turned, ordered)
    rows, wide = ordered.shape[0] // 2, sums_out.shape[1]
    grads_keep[rows:, :wide] = sums_out[0:RIDE, :]
    grads_keep[rows:, wide:] = sums_out[RIDE:, :]
    grads_one[rows:, :] = sums_out[0:RIDE, :]
    grads_two[rows:, :] = sums_out[RIDE:, :]


def slice_at(place, order):
    last = len(order) - 1
    return sum(bit * ((place >> (last - at)) & 1) for at, bit in enumerate(order))


def fill_grads(orders, me, terms, keep_out, send_outs, turned, ordered):
    width = turned.shape[0]
    half = width // 2
    share = send_outs[0].shape[1]
    column = 0
    for at_term, (left, right) in enumerate(terms):
        count = left.shape[0]
        if orders is None:
            ordered[:, :count] = left[...].T
        else:
            order = orders[at_term % len(orders)]
            parts = 1 << len(order)
            slab = width // parts
            if at_term == 0 or left is not terms[at_term - 1][0]:
                turned[:, :count] = left[...].T

            def move(place, carry, count=count, order=order):
                source = pl.multiple_of((me ^ slice_at(place, order)) * slab, 16)
                target = pl.multiple_of(place * slab, 16)
                ordered[pl.ds(target, slab), :count] = turned[pl.ds(source, slab), :count]
                return carry

            lax.fori_loop(0, parts, move, 0)
        pieces = right.shape[0] if len(right.shape) == 3 else right.shape[1] // LANES
        group = 3
        wide = group * LANES
        for index in range(pieces // group):
            if len(right.shape) == 3:
                field = jnp.concatenate([right[index * group + at] for at in range(group)], axis=1)
            else:
                field = right[:, index * wide : (index + 1) * wide]
            field = field.astype(BF16)
            keep_out[:half, column : column + wide] = dot(ordered[:half, :count], field)
            at = column % share
            send_outs[column // share][:half, at : at + wide] = dot(ordered[half:, :count], field)
            column += wide


def weight_grads(order, me_at, info, *refs):
    products = (len(refs) - 7) // 2
    lefts, rights = refs[:products], refs[products : 2 * products]
    keep_out, *send_outs = refs[2 * products : -2]
    fill_grads(order, info[me_at], tuple(zip(lefts, rights)), keep_out, send_outs, *refs[-2:])


def add_halves(pieces, joined, split, *refs):
    kept, came = refs[:2], refs[2 : 2 + 2 * pieces]
    outs = refs[2 + 2 * pieces + (2 if joined else 0) :]
    share = came[0].shape[1]
    for side in range(2):
        wide = 3 * LANES
        for start in range(0, pieces * share, wide):
            inside = start % share
            value = kept[side][:, start : start + wide] + came[2 * (start // share) + side][:, inside : inside + wide]
            if start < split:
                outs[side][:, start : start + wide] = value
            else:
                outs[2 + side][:, start - split : start - split + wide] = value
        if joined:
            outs[side][:, pieces * share :] = refs[2 + 2 * pieces + side][...]


def whole(count):
    return [pl.BlockSpec(memory_space=pltpu.VMEM)] * count


def scalars(count):
    return [pl.BlockSpec(memory_space=pltpu.SMEM)] * count


def shape(dims, kind=F32):
    return jax.ShapeDtypeStruct(dims, kind)


def after(value, *others):
    return lax.optimization_barrier((value, *others))[0]


def work(flops):
    return pl.CostEstimate(flops=flops, bytes_accessed=1, transcendentals=0)


def call(body, name, small, big, outs, scratch=(), flops=0):
    return pl.pallas_call(
        body,
        name=name,
        out_shape=outs,
        in_specs=scalars(len(small)) + whole(len(big)),
        out_specs=whole(len(outs)),
        scratch_shapes=scratch,
        cost_estimate=work(flops),
    )(*small, *big)


def per_device(
    tokens,
    neighbours,
    out_grad,
    group_sizes,
    seq_lengths,
    stretch_neighbours,
    norm_gain,
    norm_bias,
    self_qkv_w,
    self_qkv_b,
    self_out_w,
    self_out_b,
    cross_q_w,
    cross_q_b,
    cross_kv_w,
    cross_v_b,
    cross_out_w,
    cross_out_b,
    mlp_in_w,
    mlp_in_b,
    mlp_out_w,
    mlp_out_b,
):
    count, width = tokens.shape
    local = self_qkv_w.shape[2]
    hidden = mlp_in_w.shape[1]
    pairs = local // LANES
    stored, span = neighbours.shape[:2]
    slots = seq_lengths.shape[1]
    dp_size = lax.axis_size("dp")
    slab = width // dp_size
    tp_at = lax.axis_index("tp")
    dp_at = lax.axis_index("dp")
    core = dp_at % 2

    def swap(value):
        return lax.ppermute(value, "tp", [(0, 1), (1, 0)])

    def across(value, bit):
        return lax.ppermute(value, "dp", [(at, at ^ bit) for at in range(dp_size)])

    def mine(weight):
        half = weight.shape[0] // 2
        return lax.dynamic_slice_in_dim(weight, core * half, half, 0).astype(F32)

    def mine_turned(weight):
        half = weight.shape[1] // 2
        return lax.dynamic_slice_in_dim(weight, core * half, half, 1).T.astype(F32)

    def row(value):
        return value.reshape(1, -1)

    padded = count // group_sizes[0]
    info = jnp.concatenate(
        [
            jnp.stack([padded, tp_at.astype(jnp.int32), core.astype(jnp.int32)]),
            seq_lengths[0],
            dp_at.astype(jnp.int32)[None],
        ]
    )
    position = (jnp.arange(count, dtype=jnp.int32) % padded).astype(F32)
    halfway = HEAD_DIM // 2
    frequency = jnp.exp(-math.log(10000.0) * jnp.arange(halfway, dtype=F32) / halfway)
    angles = position[:, None] * jnp.tile(frequency, LANES // halfway)[None, :]
    cosine = jnp.cos(angles)
    sine = jnp.sin(angles)

    bits = [1 << at for at in range(dp_size.bit_length() - 1)]
    far_first = bits
    order = [bits] if slab % 16 == 0 else None
    mixed_order = [bits, bits, far_first] if slab % 16 == 0 else None

    def add_sent(name, kept, came, joined=(), split=None):
        rows, total = kept.shape[0] // 2, kept.shape[1]
        split = split or total
        steps = 4
        block = rows // steps

        def sides(value):
            wide = value.shape[1]
            return [
                pl.BlockSpec((block, wide), lambda i: (i, 0)),
                pl.BlockSpec((block, wide), lambda i: (i + steps, 0)),
            ]

        straight = lambda wide: pl.BlockSpec((block, wide), lambda i: (i, 0))
        first = split + sum(value.shape[1] for value in joined[:1])
        wides = [first, first] + ([total - split] * 2 if split < total else [])
        return pl.pallas_call(
            partial(add_halves, len(came), bool(joined), split),
            name=name,
            grid=(steps,),
            in_specs=[spec for value in (kept, *came) for spec in sides(value)]
            + [straight(value.shape[1]) for value in joined],
            out_specs=[straight(wide) for wide in wides],
            out_shape=[shape((rows, wide)) for wide in wides],
            cost_estimate=work(0),
        )(*[value for value in (kept, *came) for _ in range(2)], *joined)

    def sorted_halves(kept, *sent, orders=(bits,)):
        if slab % 16 == 0:
            return kept, sent
        half = width // 2
        value = jnp.concatenate([kept[:half], jnp.concatenate([piece[:half] for piece in sent], axis=1)], axis=0)
        made = []
        for part, wanted in zip(jnp.split(value, len(orders), axis=1), orders):
            places = jnp.array([slice_at(place, wanted) for place in range(dp_size)], jnp.int32) ^ dp_at
            made.append(jnp.take(part.reshape(dp_size, slab, -1), places, axis=0).reshape(part.shape))
        value = jnp.concatenate(made, axis=1)
        fresh = jnp.split(value[half:], len(sent), axis=1)
        sent = [jnp.concatenate([new, old[half:]], axis=0) for new, old in zip(fresh, sent)]
        return jnp.concatenate([value[:half], kept[half:]], axis=0), sent

    def ride_on(kept, sent, bit):
        came = across(sent, bit)
        half = kept.shape[0] // 2
        far = jnp.concatenate([kept[half:], sent[-RIDE:]], axis=0)
        return kept[:half] + came[:half], far + came[half:]

    def core_halve(halves, gate=None):
        kept, sent = halves
        came = jnp.concatenate([across(piece, 1) for piece in sent], axis=1)
        return merge(kept if gate is None else after(kept, *gate), came)

    def grads_of(total, shares, more=0):
        rows = width // 2 + more
        return (shape((rows, total)),) + (shape((rows, total // shares)),) * shares

    def turning(most):
        return [pltpu.VMEM((width, most), BF16), pltpu.VMEM((width, most), BF16)]

    def merge(kept, arrived):
        half = kept.shape[0] // 2
        return kept[:half] + arrived[:half], kept[half:] + arrived[half:]

    def halve(kept, sent, bit):
        return merge(kept, across(sent, bit))

    so_near = swap(mine(self_out_w))
    qkv_w = jnp.swapaxes(self_qkv_w, 0, 1)
    ln_one, qkv, self_mix, self_lse, mask = call(
        partial(self_forward, slots),
        "self_forward",
        (info,),
        (tokens, qkv_w, self_qkv_b, norm_gain, norm_bias, cosine, sine),
        (
            shape((count, width), BF16),
            shape((3 * pairs, count, LANES), BF16),
            shape((count, local)),
            shape((count, LANES)),
            shape((count, count)),
        ),
        flops=11_000_000_000,
    )
    self_mix_peer = swap(self_mix)
    so_far = across(so_near, 1)

    kv_w = jnp.swapaxes(cross_kv_w, 0, 1).reshape(2, width, local)
    flat_store = neighbours.reshape(stored * span, width)
    kv_bias = jnp.concatenate([jnp.zeros_like(cross_v_b), cross_v_b])
    joined_kv = jnp.concatenate([kv_w[0], kv_w[1]], axis=1)
    store_kv = (dot(flat_store, joined_kv) + kv_bias).astype(BF16)

    co_near = swap(after(mine(cross_out_w), self_mix_peer))
    hidden_one, ln_two, cross_query, cross_mix, cross_lse = call(
        partial(cross_forward, slots, span),
        "cross_forward",
        (info, stretch_neighbours),
        (
            tokens,
            self_mix,
            self_mix_peer,
            self_out_w,
            so_near,
            so_far,
            row(self_out_b),
            norm_gain,
            norm_bias,
            cross_q_w,
            row(cross_q_b),
            store_kv,
        ),
        (
            shape((count, width)),
            shape((count, width), BF16),
            shape((count, local), BF16),
            shape((count, local)),
            shape((count, LANES)),
        ),
        [pltpu.VMEM((local, width), BF16), pltpu.VMEM((count, local), F32)],
        flops=14_000_000_000,
    )
    cross_mix_peer = swap(cross_mix)
    co_far = across(co_near, 1)
    cq_near = swap(after(mine_turned(cross_q_w), cross_mix_peer))

    step = 256
    rows = lambda wide: pl.BlockSpec((step, wide), lambda i: (i, 0))
    kept = pl.BlockSpec(memory_space=pltpu.VMEM)
    own_width = width // 2
    hidden_two, ln_three, act, grad_pre, out_keep, out_send, part_three, mlp_in_b_grad = pl.pallas_call(
        feed_forward,
        name="feed_forward",
        grid=(count // step,),
        in_specs=[pl.BlockSpec(memory_space=pltpu.SMEM), rows(width), rows(local), rows(local)]
        + [kept] * 10
        + [rows(width)],
        out_specs=[
            rows(width),
            rows(width),
            rows(hidden),
            rows(hidden),
            rows(own_width),
            rows(own_width),
            rows(width),
            pl.BlockSpec((1, hidden), lambda i: (0, 0)),
        ],
        out_shape=[
            shape((count, width)),
            shape((count, width), BF16),
            shape((count, hidden), BF16),
            shape((count, hidden), BF16),
            shape((count, own_width)),
            shape((count, own_width)),
            shape((count, width)),
            shape((1, hidden)),
        ],
        scratch_shapes=[pltpu.VMEM((local, width), BF16)],
        cost_estimate=work(14_000_000_000),
    )(
        info,
        hidden_one,
        cross_mix,
        cross_mix_peer,
        cross_out_w,
        co_near,
        co_far,
        row(cross_out_b),
        norm_gain,
        norm_bias,
        mlp_in_w,
        row(mlp_in_b),
        mlp_out_w,
        row(mlp_out_b),
        out_grad,
    )
    part_three_peer = swap(part_three)
    cq_far = across(cq_near, 1)
    mlp = sorted_halves(
        *call(
            partial(weight_grads, order, 3 + slots),
            "mlp_grads",
            (info,),
            (after(out_grad, cq_near), ln_three, act, grad_pre),
            grads_of(2 * hidden, 4),
            turning(count),
            flops=0,
        )
    )
    came_mlp = [across(piece, 1) for piece in mlp[1]]
    *first, late_kept, late_sent = add_sent("add_mlp", mlp[0], came_mlp, split=7 * hidden // 4)
    (
        grad_two,
        grad_query,
        grad_query_low,
        grad_store,
        cross_sums,
        cross_q_b_grad,
        cross_v_b_grad,
        *cross_halves,
    ) = call(
        partial(cross_backward, slots, span, order),
        "cross_backward",
        (info, stretch_neighbours),
        (
            part_three,
            part_three_peer,
            after(hidden_two, first[1]),
            out_grad,
            norm_gain,
            cross_out_w,
            cross_query,
            store_kv,
            cross_lse,
            cross_mix,
            ln_two,
            flat_store,
        ),
        (
            shape((count, width)),
            shape((count, local)),
            shape((count, local), BF16),
            shape((stored * span, 2 * local), BF16),
            shape((8, width)),
            shape((1, local)),
            shape((1, local)),
            *grads_of(4 * local, 2),
        ),
        [
            pltpu.VMEM((count, local), BF16),
            pltpu.VMEM((count, local), F32),
            pltpu.VMEM((stored * span, 2 * local), F32),
            pltpu.VMEM((count, width), BF16),
            *turning(max(count, stored * span)),
        ],
        flops=17_000_000_000,
    )
    grad_query_peer = swap(grad_query)
    first = halve(*first, bits[1])

    own_kv = lax.dynamic_slice_in_dim(joined_kv, tp_at * own_width, own_width, 0)
    peer_kv = lax.dynamic_slice_in_dim(joined_kv, (1 - tp_at) * own_width, own_width, 0)
    store_send = dot_t(grad_store, peer_kv)
    store_keep = dot_t(grad_store, own_kv)
    cross = sorted_halves(*cross_halves)
    came_cross = [across(piece, 1) for piece in cross[1]]
    third = add_sent("add_cross", cross[0], came_cross, (late_kept, late_sent))
    store_back = swap(after(store_send, third[1]))

    tok_keep, both_send, *self_halves = call(
        partial(self_backward, slots, mixed_order),
        "self_backward",
        (info,),
        (
            grad_query_low,
            grad_query_peer,
            cross_q_w,
            cq_near,
            cq_far,
            hidden_one,
            after(grad_two, third[1], first[1]),
            norm_gain,
            self_out_w,
            qkv,
            self_lse,
            mask,
            cosine,
            sine,
            qkv_w,
            tokens,
            cross_sums,
            cross_q_b_grad,
            cross_v_b_grad,
            mlp_in_b_grad,
            out_send,
            self_mix,
            ln_one,
        ),
        (
            shape((count, own_width)),
            shape((count, width)),
            *grads_of(4 * local, 2, RIDE),
        ),
        [
            pltpu.VMEM((local, width), BF16),
            pltpu.VMEM((count, width), F32),
            pltpu.VMEM((pairs, count, LANES), BF16),
            pltpu.VMEM((count, LANES), F32),
            pltpu.VMEM((count, LANES), F32),
            pltpu.VMEM((256, width), F32),
            pltpu.VMEM((count, width), BF16),
            pltpu.VMEM((3 * pairs, count, LANES), BF16),
            *turning(count),
            pltpu.VMEM((2 * RIDE, width), F32),
        ],
        flops=40_000_000_000,
    )
    back = swap(both_send)

    first = halve(after(first[0], self_halves[0]), first[1], bits[2])
    third_came = across(third[1], bits[1])
    third = merge(after(third[0], self_halves[0]), third_came)
    kept, sent = sorted_halves(*self_halves, orders=(bits, far_first))
    kept = after(kept, first[1], third[1])
    half, middle = width // 4, 2 * local

    def ride_core(kept, sent):
        came = across(sent, 1)
        return kept[:half] + came[:half], kept[half:] + came[half:]

    def ride_end(kept, sent, order):
        for bit in order[:-1]:
            kept, sent = ride_on(kept, sent, bit)
        came = across(sent, order[-1])
        return kept + came[:slab], sent[-RIDE:] + came[slab:]

    near_part = ride_core(kept[:, :middle], sent[0])
    far_part = ride_core(kept[:, middle:], sent[1])
    store_back = after(store_back, near_part[1], far_part[1])
    neighbours_grad = (store_keep + store_back).astype(BF16)
    third = after(third[0], near_part[1], far_part[1]), third[1]
    first = after(first[0], near_part[1], far_part[1]), first[1]
    near_part = ride_on(*near_part, bits[1])
    far_part = ride_on(*far_part, far_first[1])
    done = near_part[1], far_part[1]
    near_part, low_sums = ride_end(*near_part, bits[2:])
    far_part, high_sums = ride_end(*far_part, far_first[2:])
    self_grads = jnp.concatenate([near_part, far_part], axis=1)
    sums = jnp.concatenate([low_sums, high_sums], axis=0)

    back = after(back, *done)
    tokens_grad = (tok_keep + back[:, :own_width]).astype(BF16)
    output = (out_keep + back[:, own_width:]).astype(BF16)

    def finish(parts, order):
        for bit in order[:-1]:
            parts = halve(*parts, bit)
        return after(parts[0], *done) + across(parts[1], order[-1])

    mlp_grads = finish(first, bits[3:])
    third = finish(third, bits[2:])
    cross_grads = third[:, : 4 * local]
    mlp_out_w_grad = mlp_grads[:, :hidden]
    mlp_in_w_grad = jnp.concatenate([mlp_grads[:, hidden:], third[:, 4 * local :]], axis=1)

    shared = 0.5 * sums[2:9]
    shared = jnp.concatenate([sums[0:2], shared], axis=0)
    shared = shared + swap(shared)
    alone = sums[9:].reshape(-1)
    return (
        output,
        tokens_grad,
        neighbours_grad.reshape(stored, span, own_width),
        jnp.stack([shared[0], shared[2], shared[5]]),
        jnp.stack([shared[1], shared[3], shared[6]]),
        self_grads[:, local:].reshape(-1, 3, local),
        alone[: 3 * local].reshape(3, local),
        self_grads[:, :local].T,
        shared[4],
        cross_grads[:, local : 2 * local],
        alone[3 * local : 4 * local],
        cross_grads[:, 2 * local :].reshape(-1, 2, local),
        alone[4 * local : 5 * local],
        cross_grads[:, :local].T,
        shared[7],
        mlp_in_w_grad,
        alone[5 * local : 5 * local + hidden],
        mlp_out_w_grad.T,
        shared[8],
    )


def solution(mesh):
    placed = (
        P("dp", None),
        P("dp", None, None),
        P("dp", None),
        P("dp"),
        P("dp", None),
        P("dp", None),
        P(),
        P(),
        P(None, None, "tp"),
        P(None, "tp"),
        P("tp", None),
        P(),
        P(None, "tp"),
        P("tp"),
        P(None, None, "tp"),
        P("tp"),
        P("tp", None),
        P(),
        P(None, "tp"),
        P("tp"),
        P("tp", None),
        P(),
    )
    return jax.shard_map(
        per_device,
        mesh=mesh,
        in_specs=placed,
        out_specs=(
            P("dp", "tp"),
            P("dp", "tp"),
            P("dp", None, "tp"),
            P(),
            P(),
            P("dp", None, "tp"),
            P(None, "tp"),
            P("tp", "dp"),
            P(),
            P("dp", "tp"),
            P("tp"),
            P("dp", None, "tp"),
            P("tp"),
            P("tp", "dp"),
            P(),
            P("dp", "tp"),
            P("tp"),
            P("tp", "dp"),
            P(),
        ),
        check_vma=False,
    )
```
